256 devices in a mesh: row: 4 (over y), col: 64 (over z, x, core).
Axes of the slice: x: 4, y: 4, z: 8, core: 2. Of those that a mesh axis runs over, the one named last changes fastest.
Arguments:
- queries: bfloat16 [1024, 4096], P(('row', 'col')), may hold values from -1.25 to 1.25
- passages: bfloat16 [32768, 4096], P(('col', 'row')), may hold values from -0.375 to 0.375
- positives: int32 [1024], P('row'), may hold values from 0 to 32767, as said below
- hard_negatives: int32 [1024, 7], P('row'), may hold values from 0 to 32767, as said below
- thresholds: float32 [1024], P('row'), may hold values from 0.1 to 2
Outputs:
- row_losses: float32 [1024], P(('row', 'col'))
- grad_queries: float32 [1024, 4096], P(('row', 'col'))
- grad_passages: float32 [32768, 4096], P(('col', 'row'))
The draws below stay inside these ranges and needn't reach their ends.
Inputs may be any that keep to these rules, and one draw needn't show every extreme that they name: `positives`: each query's positive passage. `hard_negatives`: passages mined for each query; ids may repeat or equal the query's positive.
All inputs are finite; a program needn't handle non-finite values.
Results may differ from the reference program's by a relative error of at most 0.0023.
Values may be sent and summed in bfloat16 or wider, within the bound.
No kernel may reach another device: no remote copies, remote signals or barrier semaphores. Data moves between devices by JAX's collectives and lax.ppermute only.
A program may use at most 64 MiB of HBM per device.

```python
import math
import jax
import jax.numpy as jnp
from jax import lax

D = 4096
NEGS = 7
NQ = 1024
NP = 32768


def integer_tables(key):
    positives = jax.random.randint(jax.random.fold_in(key, 11), (NQ,), 0, NP)
    mined_ids = jax.random.randint(jax.random.fold_in(key, 12), (NQ, NEGS), 0, NP)
    return (positives, mined_ids)


def log_even(key, shape, lower, upper):
    return jnp.exp(jax.random.uniform(key, shape, jnp.float32, math.log(lower), math.log(upper)))


def embedding_tables(key):
    positives, mined_ids = integer_tables(key)
    unit_scale = D ** (-0.5)
    passage_noise = jax.random.truncated_normal(jax.random.fold_in(key, 21), -6.0, 6.0, (NP, D), jnp.float32) * unit_scale
    scales = log_even(jax.random.fold_in(key, 22), (NP, 1), 0.7, 1.4)
    passages = passage_noise * scales
    query_noise = jax.random.truncated_normal(jax.random.fold_in(key, 24), -6.0, 6.0, (NQ, D), jnp.float32) * unit_scale
    linked = 0.06 * passages[positives] + 0.05 * jnp.sum(passages[mined_ids], axis=1)
    query_scale = log_even(jax.random.fold_in(key, 25), (NQ, 1), 0.6, 1.6)
    queries = (query_noise + linked) * query_scale
    queries = jnp.clip(queries, -80.0 * unit_scale, 80.0 * unit_scale)
    passages = jnp.clip(passages, -24.0 * unit_scale, 24.0 * unit_scale)
    return (queries, passages)


def draw_queries(key, part):
    return embedding_tables(key)[0].astype(jnp.bfloat16)


def draw_passages(key, part):
    return embedding_tables(key)[1].astype(jnp.bfloat16)


def draw_positives(key, part):
    return integer_tables(key)[0]


def draw_hard_negatives(key, part):
    return integer_tables(key)[1]


def level_of(stream_key, extent, cuts, low, largest):
    loudness, own = 1.0, jax.random.fold_in(stream_key, 6)
    for axis_at, blocks in cuts:
        draws = jnp.exp(jax.random.uniform(jax.random.fold_in(own, axis_at), (blocks,), jnp.float32, low / len(cuts), largest / len(cuts)))
        loudness = loudness * jnp.repeat(draws, extent[axis_at] // blocks).reshape([-1 if axis == axis_at else 1 for axis in range(len(extent))])
    return loudness


def setup_inputs(seed: int = 0) -> dict:
    keys = jax.random.split(jax.random.key(seed), 6)
    return {
        "queries": draw_queries(jax.random.fold_in(keys[5], 71), 0),
        "passages": draw_passages(jax.random.fold_in(keys[5], 71), 0),
        "positives": draw_positives(jax.random.fold_in(keys[5], 71), 0),
        "hard_negatives": draw_hard_negatives(jax.random.fold_in(keys[5], 71), 0),
        "thresholds": jnp.clip(jnp.exp(math.log(2.0) - 2.9957323 * jax.random.uniform(keys[4], (NQ,), jnp.float32) ** level_of(keys[4], (NQ,), ((0, 4),), -0.2, 0.2)), 0.1, 2.0),
    }


inv_temp = 50.0
sharpness = 4.0


def reference(queries, passages, positives, hard_negatives, thresholds):
    scores = jnp.dot(queries, passages.T, preferred_element_type=jnp.float32) * inv_temp
    columns = lax.iota(jnp.int32, passages.shape[0])
    positive_mask = positives[:, None] == columns[None, :]
    kept_mask = positive_mask
    for mined_slot in range(NEGS):
        kept_mask = kept_mask | (hard_negatives[:, mined_slot:mined_slot + 1] == columns[None, :])
    picked = jnp.sum(jnp.where(positive_mask, scores, 0.0), axis=1)
    penalty = jax.nn.softplus(sharpness * (scores - picked[:, None] - thresholds[:, None]))
    logits = jnp.where(kept_mask, scores, scores - penalty)
    row_top = jnp.max(logits, axis=1)
    shifted = jnp.exp(logits - row_top[:, None])
    denominator = jnp.sum(shifted, axis=1)
    row_losses = row_top + jnp.log(denominator) - picked
    grad_scores = ((shifted / denominator[:, None] - positive_mask.astype(jnp.float32)) * inv_temp).astype(jnp.bfloat16)
    grad_queries = jnp.dot(grad_scores, passages, preferred_element_type=jnp.float32)
    grad_passages = jnp.dot(grad_scores.T, queries, preferred_element_type=jnp.float32)
    return row_losses, grad_queries, grad_passages
```

```python
import functools

import jax
import jax.numpy as jnp
from jax import lax
from jax.experimental import pallas as pl
from jax.experimental.pallas import tpu as pltpu
from jax.sharding import Mesh
from jax.sharding import PartitionSpec as P

Y, Z, X, CORE = "row", "col_0", "col_1", "col_2"
COL = (Z, X, CORE)
ROW_COL = (Y, Z, X, CORE)
COL_ROW = (Z, X, CORE, Y)

inv_temp = 50.0
sharpness = 4.0
LOWEST = -3.0e38
F32, BF16 = jnp.float32, jnp.bfloat16
TILE = 512


def shifted(value, axis, step):
    n = lax.axis_size(axis)
    return lax.ppermute(value, axis, [(i, (i + step) % n) for i in range(n)])


def copies(value, axis):
    n = lax.axis_size(axis)
    return lax.all_to_all(jnp.broadcast_to(value, (n, *value.shape)), axis, 0, 0, tiled=True)


def shape(dims, dtype):
    return jax.ShapeDtypeStruct(dims, dtype)


def call(body, outs, args, flops=0, scalars=0):
    size = sum(a.size * a.dtype.itemsize for a in (*args, *outs))
    spaces = [pltpu.SMEM] * scalars + [pltpu.VMEM] * (len(args) - scalars)
    return pl.pallas_call(
        body,
        out_shape=outs,
        in_specs=[pl.BlockSpec(memory_space=s) for s in spaces],
        out_specs=[pl.BlockSpec(memory_space=pltpu.VMEM)] * len(outs),
        cost_estimate=pl.CostEstimate(flops=flops, bytes_accessed=size, transcendentals=0),
        compiler_params=pltpu.CompilerParams(vmem_limit_bytes=48 << 20),
    )(*args)


def eye():
    rows = lax.broadcasted_iota(jnp.int32, (128, 128), 0)
    return rows == lax.broadcasted_iota(jnp.int32, (128, 128), 1)


def as_row(column, diagonal):
    return jnp.sum(jnp.where(diagonal, column, 0.0), axis=0, keepdims=True)


def as_column(row, diagonal):
    return jnp.sum(jnp.where(diagonal, row, 0.0), axis=1, keepdims=True)


def in_place(core, own, other):
    return jnp.where(core == 0, own, other), jnp.where(core == 0, other, own)


def mask_body(meta_ref, columns_ref, code_ref):
    columns = columns_ref[0:1, :]
    for block in range(2):
        rows = slice(128 * block, 128 * block + 128)
        meta = meta_ref[rows, :]
        kept = meta[:, 1:2] == columns
        for slot in range(2, 8):
            kept = kept | (meta[:, slot : slot + 1] == columns)
        code_ref[rows, :] = jnp.where(meta[:, 0:1] == columns, 2.0, jnp.where(kept, 1.0, 0.0))


def tiles(width, body):
    def step(k, _):
        body(pl.ds(pl.multiple_of(k * TILE, TILE), TILE))
        return 0

    lax.fori_loop(0, width // TILE, step, 0)


def score_body(*refs):
    own, other = refs[0:2]
    pool, scores = refs[2:-1], refs[-1]
    scores[...] = jnp.zeros_like(scores)
    contract = (((1,), (1,)), ((), ()))

    def step(at):
        block = jnp.concatenate([p[:, at] for p in pool], axis=0)
        for k, q in ((0, own), (1, other)):
            scores[128 * k : 128 * k + 128, :] += lax.dot_general(
                q[:, at], block, contract, preferred_element_type=F32
            )

    tiles(own.shape[1], step)


def stat_body(core_ref, first, last, code, table):
    diagonal = eye()
    found = []
    for k in range(2):
        rows = slice(128 * k, 128 * k + 128)
        block = jnp.concatenate([first[rows, :], last[rows, :]], axis=1) * inv_temp
        flags = code[rows, :]
        positive = jnp.max(jnp.where(flags == 2.0, block, LOWEST), axis=1, keepdims=True)
        kept = jnp.max(jnp.where(flags > 0.0, block, LOWEST), axis=1, keepdims=True)
        found.append((as_row(positive, diagonal), as_row(kept, diagonal)))
    core = core_ref[0]
    lines = [*in_place(core, found[0][0], found[1][0]), *in_place(core, found[0][1], found[1][1])]
    table[...] = jnp.broadcast_to(jnp.concatenate(lines, axis=0)[None], table.shape)


def soft_body(core_ref, table, meta_ref, code, first, last, weights, totals, stats):
    core = core_ref[0]
    merged = jnp.max(table[...], axis=0)
    lines = [
        *in_place(core, merged[0:1], merged[1:2]),
        *in_place(core, merged[2:3], merged[3:4]),
    ]
    diagonal = eye()
    sums, tops = [], []
    for k in range(2):
        rows = slice(128 * k, 128 * k + 128)
        picked = as_column(lines[k], diagonal)
        kept = as_column(lines[2 + k], diagonal)
        margin = meta_ref[rows, 8:9]
        ceiling = jnp.maximum(kept, picked + margin)
        block = jnp.concatenate([first[rows, :], last[rows, :]], axis=1) * inv_temp
        over = sharpness * (block - picked - margin)
        penalty = jnp.maximum(over, 0.0) + jnp.log(1.0 + jnp.exp(-jnp.abs(over)))
        logits = jnp.where(code[rows, :] > 0.0, block, block - penalty)
        weight = jnp.exp(logits - ceiling)
        weights[rows, :] = weight
        sums.append(as_row(jnp.sum(weight, axis=1, keepdims=True), diagonal))
        tops.append(as_row(ceiling, diagonal) - lines[k])
    lines = in_place(core, *sums)
    totals[...] = jnp.broadcast_to(jnp.concatenate(lines, axis=0)[None], totals.shape)
    stats[...] = jnp.broadcast_to(tops[0], stats.shape)


def grad_body(core_ref, table, stats, code, weights, own, other, grads, losses, low, high):
    merged = jnp.sum(table[...], axis=0)
    lines = in_place(core_ref[0], merged[0:1], merged[1:2])
    losses[...] = stats[...] + jnp.log(lines[0])
    diagonal = eye()
    for k in range(2):
        rows = slice(128 * k, 128 * k + 128)
        total = as_column(lines[k], diagonal)
        positive = jnp.where(code[rows, :] == 2.0, 1.0, 0.0)
        grads[rows, :] = ((weights[rows, :] / total - positive) * inv_temp).astype(BF16)
    block = grads[:, 384:512].T

    def step(at):
        pool = jnp.concatenate([own[:, at], other[:, at]], axis=0)
        out = jnp.dot(block, pool, preferred_element_type=F32).astype(BF16)
        low[:, at] = out[:64]
        high[:, at] = out[64:]

    tiles(own.shape[1], step)


def passage_body(grads, own, other, here, back, ahead):
    block = grads[:, 0:384].T

    def step(at):
        pool = jnp.concatenate([own[:, at], other[:, at]], axis=0)
        out = jnp.dot(block, pool, preferred_element_type=F32)
        here[:, at] = out[0:128]
        back[:, at] = out[128:256]
        ahead[:, at] = out[256:384]

    tiles(own.shape[1], step)


def query_body(grads, here, back, ahead, low, high, own, other):
    block = grads[...]

    def step(at):
        pool = jnp.concatenate([p[:, at] for p in (here, back, ahead, low, high)], axis=0)
        out = jnp.dot(block, pool, preferred_element_type=F32)
        own[:, at] = out[:128]
        other[:, at] = out[128:]

    tiles(here.shape[1], step)


def on_device(queries, passages, positives, hard_negatives, thresholds):
    rows, width = queries.shape
    count = passages.shape[0]
    depth, breadth, ring = lax.axis_size(Z), lax.axis_size(X), lax.axis_size(Y)
    core, far, across, along = (lax.axis_index(a) for a in (CORE, Z, X, Y))
    flag = core.reshape(1)
    half = count // 2

    back, ahead = shifted(passages, Y, 1), shifted(passages, Y, -1)
    line = copies(queries, Z).reshape(depth * rows, width)
    own = copies(line, X).reshape(-1, width)
    low, high = shifted(back[:half], Y, 1), shifted(ahead[half:], Y, -1)
    other = shifted(own, CORE, 1)
    plane = own.shape[0]
    total, pool = 2 * plane, ring * count

    meta = jnp.concatenate(
        [positives[None, :].astype(F32), hard_negatives.T.astype(F32), thresholds[None, :]], axis=0
    )
    meta = meta.reshape(9, depth, breadth, 2, rows)
    meta = jnp.transpose(meta, (3, 2, 1, 4, 0)).reshape(2, plane, 9)
    meta = jnp.where(core == 0, meta, jnp.flip(meta, 0)).reshape(total, 9)
    meta = jnp.pad(meta, ((0, 0), (0, 7)))
    steps = jnp.array([0, 1, 3, 2], jnp.int32)
    base = ((far * breadth + across) * 2 + core) * ring + (along - steps) % ring
    columns = (base[:, None] * count + lax.iota(jnp.int32, count)[None, :]).astype(F32)
    columns = jnp.broadcast_to(columns.reshape(1, pool), (8, pool))
    code = call(mask_body, [shape((total, pool), F32)], [meta, columns])[0]

    first = call(
        score_body,
        [shape((total, 3 * count), F32)],
        [own, other, passages, back, ahead],
        flops=2 * total * 3 * count * width,
    )[0]
    last = call(
        score_body,
        [shape((total, count), F32)],
        [own, other, low, high],
        flops=2 * total * count * width,
    )[0]
    members = depth * breadth * 2
    table = call(stat_body, [shape((members, 4, plane), F32)], [flag, first, last, code], scalars=1)[0]
    table = lax.all_to_all(table, COL, 0, 0, tiled=True)
    weights, table, stats = call(
        soft_body,
        [shape((total, pool), F32), shape((members, 2, plane), F32), shape((8, plane), F32)],
        [flag, table, meta, code, first, last],
        scalars=1,
    )
    table = lax.all_to_all(table, COL, 0, 0, tiled=True)
    grads, losses, low_sum, high_sum = call(
        grad_body,
        [shape((total, pool), BF16), shape((8, plane), F32)] + [shape((half, width), BF16)] * 2,
        [flag, table, stats, code, weights, own, other],
        flops=2 * total * count * width,
        scalars=1,
    )
    low_sum, high_sum = shifted(low_sum, Y, -1), shifted(high_sum, Y, 1)

    own_sum, other_sum = call(
        query_body,
        [shape((plane, width), F32)] * 2,
        [grads, passages, back, ahead, low, high],
        flops=2 * total * pool * width,
    )
    own_sum = own_sum + shifted(other_sum, CORE, 1)
    own_sum = lax.psum_scatter(own_sum, X, scatter_dimension=0, tiled=True)
    grad_queries = lax.psum_scatter(own_sum, Z, scatter_dimension=0, tiled=True)

    here, back_sum, ahead_sum = call(
        passage_body,
        [shape((count, width), F32)] * 3,
        [grads, own, other],
        flops=2 * total * 3 * count * width,
    )
    back_sum = jnp.concatenate([back_sum[:half] + low_sum.astype(F32), back_sum[half:]], axis=0)
    ahead_sum = jnp.concatenate([ahead_sum[:half], ahead_sum[half:] + high_sum.astype(F32)], axis=0)
    back_sum, ahead_sum = shifted(back_sum.astype(BF16), Y, -1), shifted(ahead_sum.astype(BF16), Y, 1)
    grad_passages = here + back_sum.astype(F32) + ahead_sum.astype(F32)

    at = (across * depth + far) * rows
    row_losses = lax.dynamic_slice_in_dim(losses[0], at, rows, 0)
    return row_losses, grad_queries, grad_passages


def solution(mesh):
    torus = Mesh(mesh.devices.reshape(mesh.shape[Y], 8, 4, 2), ROW_COL)
    in_specs = (P(ROW_COL, None), P(COL_ROW, None), P(Y), P(Y, None), P(Y))
    out_specs = (P(ROW_COL), P(ROW_COL, None), P(COL_ROW, None))
    return jax.shard_map(
        on_device, mesh=torus, in_specs=in_specs, out_specs=out_specs, check_vma=False
    )
```

```python
import functools

import jax
import jax.numpy as jnp
from jax import lax
from jax.experimental import pallas as pl
from jax.experimental.pallas import tpu as pltpu
from jax.sharding import Mesh
from jax.sharding import PartitionSpec as P

Y, Z, X, CORE = "row", "col_0", "col_1", "col_2"
COL = (Z, X, CORE)
ROW_COL = (Y, Z, X, CORE)
COL_ROW = (Z, X, CORE, Y)

inv_temp = 50.0
sharpness = 4.0
LOWEST = -3.0e38
F32, BF16 = jnp.float32, jnp.bfloat16
TILE = 512


def shifted(value, axis, step):
    n = lax.axis_size(axis)
    return lax.ppermute(value, axis, [(i, (i + step) % n) for i in range(n)])


def copies(value, axis):
    n = lax.axis_size(axis)
    return lax.all_to_all(jnp.broadcast_to(value, (n, *value.shape)), axis, 0, 0, tiled=True)


def shape(dims, dtype):
    return jax.ShapeDtypeStruct(dims, dtype)


def call(body, outs, args, flops=0, scalars=0, tiled=(), scratch=()):
    size = sum(a.size * a.dtype.itemsize for a in (*args, *outs))
    specs = []
    for k, a in enumerate((*args, *outs)):
        if k < scalars:
            specs.append(pl.BlockSpec(memory_space=pltpu.SMEM))
        elif k in tiled:
            specs.append(pl.BlockSpec((a.shape[0], TILE), lambda i: (0, i)))
        else:
            specs.append(pl.BlockSpec(a.shape, lambda i, n=len(a.shape): (0,) * n))
    steps = (*args, *outs)[tiled[0]].shape[1] // TILE if tiled else 1
    return pl.pallas_call(
        body,
        grid=(steps,),
        out_shape=outs,
        in_specs=specs[: len(args)],
        out_specs=specs[len(args) :],
        scratch_shapes=scratch,
        cost_estimate=pl.CostEstimate(flops=flops, bytes_accessed=size, transcendentals=0),
        compiler_params=pltpu.CompilerParams(vmem_limit_bytes=24 << 20),
    )(*args)


def swapped(core, row):
    half = row.shape[1] // 2
    return jnp.where(core == 0, row, jnp.concatenate([row[:, half:], row[:, :half]], axis=1))


def on_step(k):
    return pl.when(pl.program_id(0) == k)


def products(own, other, pool, scores):
    @on_step(0)
    def _():
        scores[...] = jnp.zeros_like(scores)

    rows = jnp.concatenate([p[...] for p in pool], axis=0)
    columns = jnp.concatenate([own[...], other[...]], axis=0)
    scores[...] += lax.dot_general(
        rows, columns, (((1,), (1,)), ((), ())), preferred_element_type=F32
    )


def score_body(own, other, here, back, ahead, scores):
    products(own, other, (here, back, ahead), scores)


def stat_body(place, own, other, low, high, first, ids, last, code, table):
    products(own, other, (low, high), last)

    @pl.when(pl.program_id(0) == pl.num_programs(0) - 1)
    def _():
        positive, kept = [], []
        for k in range(4):
            rows = slice(128 * k, 128 * k + 128)
            block = (last[...] if k == 3 else first[rows, :]) * inv_temp
            column = place[1 + k] + lax.broadcasted_iota(jnp.int32, block.shape, 0)
            is_positive = column == ids[0:1, :]
            is_kept = is_positive
            for slot in range(1, 8):
                is_kept = is_kept | (column == ids[slot : slot + 1, :])
            code[rows, :] = jnp.where(is_positive, 2.0, jnp.where(is_kept, 1.0, 0.0))
            positive.append(jnp.max(jnp.where(is_positive, block, LOWEST), axis=0, keepdims=True))
            kept.append(jnp.max(jnp.where(is_kept, block, LOWEST), axis=0, keepdims=True))
        lines = [swapped(place[0], functools.reduce(jnp.maximum, v)) for v in (positive, kept)]
        table[...] = jnp.broadcast_to(jnp.concatenate(lines, axis=0)[None], table.shape)


def soft_body(place, table, margin_ref, code, first, last, weights, totals, stats):
    merged = swapped(place[0], jnp.max(table[...], axis=0))
    picked, kept = merged[0:1], merged[1:2]
    margin = margin_ref[0:1, :]
    ceiling = jnp.maximum(kept, picked + margin)
    sums = []
    for k in range(4):
        rows = slice(128 * k, 128 * k + 128)
        block = (last[...] if k == 3 else first[rows, :]) * inv_temp
        over = sharpness * (block - picked - margin)
        penalty = jnp.maximum(over, 0.0) + jnp.log(1.0 + jnp.exp(-jnp.abs(over)))
        logits = jnp.where(code[rows, :] > 0.0, block, block - penalty)
        weight = jnp.exp(logits - ceiling)
        weights[rows, :] = weight
        sums.append(jnp.sum(weight, axis=0, keepdims=True))
    total = swapped(place[0], functools.reduce(jnp.add, sums))
    totals[...] = jnp.broadcast_to(total[None], totals.shape)
    stats[...] = jnp.broadcast_to(ceiling - picked, stats.shape)


def grad_body(place, table, stats, code, weights, own, other, grads, losses, low, high):
    @on_step(0)
    def _():
        total = swapped(place[0], jnp.sum(table[...], axis=0))
        losses[...] = stats[...] + jnp.log(total)
        for k in range(4):
            rows = slice(128 * k, 128 * k + 128)
            positive = jnp.where(code[rows, :] == 2.0, 1.0, 0.0)
            grads[rows, :] = ((weights[rows, :] / total - positive) * inv_temp).astype(BF16)

    columns = jnp.concatenate([own[...], other[...]], axis=0)
    out = jnp.dot(grads[384:512, :], columns, preferred_element_type=F32).astype(BF16)
    low[...] = out[:64]
    high[...] = out[64:]


def passage_body(grads, own, other, low, high, here, back, ahead):
    columns = jnp.concatenate([own[...], other[...]], axis=0)
    out = jnp.dot(grads[0:384, :], columns, preferred_element_type=F32)
    here[...] = out[0:128]
    back[0:64, :] = (out[128:192] + low[...].astype(F32)).astype(BF16)
    back[64:128, :] = out[192:256].astype(BF16)
    ahead[0:64, :] = out[256:320].astype(BF16)
    ahead[64:128, :] = (out[320:384] + high[...].astype(F32)).astype(BF16)


def query_body(grads, here, back, ahead, low, high, own, other, turned):
    @on_step(0)
    def _():
        turned[...] = grads[...].T

    rows = jnp.concatenate([p[...] for p in (here, back, ahead, low, high)], axis=0)
    out = jnp.dot(turned[...], rows, preferred_element_type=F32)
    own[...] = out[:128]
    other[...] = out[128:]


def join_body(own, arrived, exact, sent):
    total = own[...] + arrived[...]
    exact[...] = total
    sent[...] = total.astype(BF16)


def spread_sum(sent, exact, axis):
    n = lax.axis_size(axis)
    mine = lax.axis_index(axis)
    parts = lax.all_to_all(sent.reshape(n, -1, sent.shape[-1]), axis, 0, 0, tiled=True)
    rest = jnp.where((lax.iota(jnp.int32, n) == mine)[:, None, None], 0.0, parts.astype(F32))
    own = lax.dynamic_index_in_dim(exact.reshape(parts.shape), mine, 0, keepdims=False)
    return jnp.sum(rest, axis=0) + own


def on_device(queries, passages, positives, hard_negatives, thresholds):
    rows, width = queries.shape
    count = passages.shape[0]
    depth, breadth, ring = lax.axis_size(Z), lax.axis_size(X), lax.axis_size(Y)
    core, far, across, along = (lax.axis_index(a) for a in (CORE, Z, X, Y))
    half = count // 2

    back, ahead = shifted(passages, Y, 1), shifted(passages, Y, -1)
    line = copies(queries, Z)
    line, back, ahead = lax.optimization_barrier((line, back, ahead))
    low, high = shifted(back[:half], Y, 1), shifted(ahead[half:], Y, -1)
    own = copies(line.reshape(depth * rows, width), X)
    own, low, high = lax.optimization_barrier((own, low, high))
    own = own.reshape(-1, width)
    other = shifted(own, CORE, 1)
    plane = own.shape[0]
    total, pool = 2 * plane, ring * count

    def ordered(table):
        table = table.reshape(-1, depth, breadth, 2, rows)
        table = jnp.transpose(table, (0, 3, 2, 1, 4)).reshape(-1, 2, plane)
        return jnp.where(core == 0, table, jnp.flip(table, 1)).reshape(-1, total)

    ids = ordered(jnp.concatenate([positives[None, :], hard_negatives.T], axis=0))
    margin = ordered(jnp.broadcast_to(thresholds, (8, total)))
    steps = jnp.array([0, 1, 3, 2], jnp.int32)
    base = (((far * breadth + across) * 2 + core) * ring + (along - steps) % ring) * count
    place = jnp.concatenate([core.reshape(1), base]).astype(jnp.int32)

    members = depth * breadth * 2
    first = call(
        score_body,
        [shape((3 * count, total), F32)],
        [own, other, passages, back, ahead],
        flops=2 * total * 3 * count * width,
        tiled=(0, 1, 2, 3, 4),
    )[0]
    last, code, table = call(
        stat_body,
        [shape((count, total), F32), shape((pool, total), F32), shape((members, 2, total), F32)],
        [place, own, other, low, high, first, ids],
        flops=2 * total * count * width,
        scalars=1,
        tiled=(1, 2, 3, 4),
    )
    table = lax.all_to_all(table, COL, 0, 0, tiled=True)
    weights, table, stats = call(
        soft_body,
        [shape((pool, total), F32), shape((members, 1, total), F32), shape((8, total), F32)],
        [place, table, margin, code, first, last],
        scalars=1,
    )
    table = lax.all_to_all(table, COL, 0, 0, tiled=True)
    grads, losses, low_sum, high_sum = call(
        grad_body,
        [shape((pool, total), BF16), shape((8, total), F32)] + [shape((half, width), BF16)] * 2,
        [place, table, stats, code, weights, own, other],
        flops=2 * total * count * width,
        scalars=1,
        tiled=(5, 6, 9, 10),
    )
    low_sum, high_sum = shifted(low_sum, Y, -1), shifted(high_sum, Y, 1)

    own_sum, other_sum = call(
        query_body,
        [shape((plane, width), F32)] * 2,
        [grads, passages, back, ahead, low, high],
        flops=2 * total * pool * width,
        tiled=(1, 2, 3, 4, 5, 6, 7),
        scratch=[pltpu.VMEM((total, pool), BF16)],
    )
    exact, sent = call(
        join_body,
        [shape((plane, width), F32), shape((plane, width), BF16)],
        [own_sum, shifted(other_sum, CORE, 1)],
        tiled=(0, 1, 2, 3),
    )
    exact = spread_sum(sent, exact, X)
    grad_queries = spread_sum(exact.astype(BF16), exact, Z)

    here, back_sum, ahead_sum = call(
        passage_body,
        [shape((count, width), F32)] + [shape((count, width), BF16)] * 2,
        [grads, own, other, low_sum, high_sum],
        flops=2 * total * 3 * count * width,
        tiled=(1, 2, 3, 4, 5, 6, 7),
    )
    back_sum, ahead_sum = shifted(back_sum, Y, -1), shifted(ahead_sum, Y, 1)
    grad_passages = here + back_sum.astype(F32) + ahead_sum.astype(F32)

    at = (across * depth + far) * rows
    row_losses = lax.dynamic_slice_in_dim(losses[0], at, rows, 0)
    return row_losses, grad_queries, grad_passages


def solution(mesh):
    torus = Mesh(mesh.devices.reshape(mesh.shape[Y], 8, 4, 2), ROW_COL)
    in_specs = (P(ROW_COL, None), P(COL_ROW, None), P(Y), P(Y, None), P(Y))
    out_specs = (P(ROW_COL), P(ROW_COL, None), P(COL_ROW, None))
    return jax.shard_map(
        on_device, mesh=torus, in_specs=in_specs, out_specs=out_specs, check_vma=False
    )
```

```python
import functools

import jax
import jax.numpy as jnp
from jax import lax
from jax.experimental import pallas as pl
from jax.experimental.pallas import tpu as pltpu
from jax.sharding import Mesh
from jax.sharding import PartitionSpec as P

Y, Z, X, CORE = "row", "col_0", "col_1", "col_2"
COL = (Z, X, CORE)
ROW_COL = (Y, Z, X, CORE)
COL_ROW = (Z, X, CORE, Y)

inv_temp = 50.0
sharpness = 4.0
LOWEST = -3.0e38
F32, BF16 = jnp.float32, jnp.bfloat16
TILE = 1024


def shifted(value, axis, step):
    n = lax.axis_size(axis)
    return lax.ppermute(value, axis, [(i, (i + step) % n) for i in range(n)])


def copies(value, axis):
    n = lax.axis_size(axis)
    return lax.all_to_all(jnp.broadcast_to(value, (n, *value.shape)), axis, 0, 0, tiled=True)


def shape(dims, dtype):
    return jax.ShapeDtypeStruct(dims, dtype)


def call(body, outs, args, flops=0, scalars=0, tiled=(), scratch=()):
    size = sum(a.size * a.dtype.itemsize for a in (*args, *outs))
    specs = []
    for k, a in enumerate((*args, *outs)):
        if k < scalars:
            specs.append(pl.BlockSpec(memory_space=pltpu.SMEM))
        elif k in tiled:
            specs.append(pl.BlockSpec((a.shape[0], TILE), lambda i: (0, i)))
        else:
            specs.append(pl.BlockSpec(a.shape, lambda i, n=len(a.shape): (0,) * n))
    steps = (*args, *outs)[tiled[0]].shape[1] // TILE if tiled else 1
    return pl.pallas_call(
        body,
        grid=(steps,),
        out_shape=outs,
        in_specs=specs[: len(args)],
        out_specs=specs[len(args) :],
        scratch_shapes=scratch,
        cost_estimate=pl.CostEstimate(flops=flops, bytes_accessed=size, transcendentals=0),
        compiler_params=pltpu.CompilerParams(vmem_limit_bytes=24 << 20),
    )(*args)


def swapped(core, row):
    half = row.shape[1] // 2
    return jnp.where(core == 0, row, jnp.concatenate([row[:, half:], row[:, :half]], axis=1))


def on_step(k):
    return pl.when(pl.program_id(0) == k)


def marks(place, ids, k, lines):
    column = place[1 + k] + lax.broadcasted_iota(jnp.int32, (128, ids.shape[1]), 0)
    found = [column == ids[slot : slot + 1, :] for slot in range(lines)]
    return found[0], functools.reduce(jnp.logical_or, found)


def score_body(place, own, other, *refs):
    pool, ids, scores, table = refs[:7], *refs[7:]

    @on_step(0)
    def _():
        scores[...] = jnp.zeros_like(scores)

    rows = jnp.concatenate([p[...] for p in pool], axis=0)
    columns = jnp.concatenate([own[...], other[...]], axis=0)
    scores[...] += lax.dot_general(
        rows, columns, (((1,), (1,)), ((), ())), preferred_element_type=F32
    )

    @pl.when(pl.program_id(0) == pl.num_programs(0) - 1)
    def _():
        tops = [[], []]
        for k in range(4):
            rows = slice(128 * k, 128 * k + 128)
            block = scores[rows, :] * inv_temp
            scores[rows, :] = block
            for top, mark in zip(tops, marks(place, ids, k, 8)):
                top.append(jnp.max(jnp.where(mark, block, LOWEST), axis=0, keepdims=True))
        lines = [swapped(place[0], functools.reduce(jnp.maximum, top)) for top in tops]
        table[...] = jnp.broadcast_to(jnp.concatenate(lines, axis=0)[None], table.shape)


def soft_body(place, table, margin_ref, ids, scores, weights, totals, stats):
    merged = swapped(place[0], jnp.max(table[...], axis=0))
    picked, kept = merged[0:1], merged[1:2]
    margin = margin_ref[0:1, :]
    ceiling = jnp.maximum(kept, picked + margin)
    sums = []
    for k in range(4):
        rows = slice(128 * k, 128 * k + 128)
        block = scores[rows, :]
        over = sharpness * (block - picked - margin)
        penalty = jnp.maximum(over, 0.0) + jnp.log(1.0 + jnp.exp(-jnp.abs(over)))
        logits = jnp.where(marks(place, ids, k, 8)[1], block, block - penalty)
        weight = jnp.exp(logits - ceiling)
        weights[rows, :] = weight
        sums.append(jnp.sum(weight, axis=0, keepdims=True))
    total = swapped(place[0], functools.reduce(jnp.add, sums))
    totals[...] = jnp.broadcast_to(total[None], totals.shape)
    stats[...] = jnp.broadcast_to(ceiling - picked, stats.shape)


def grad_body(place, table, stats, ids, weights, own, other, *refs):
    pool, outs, (grads, turned) = refs[:7], refs[7:17], refs[17:]
    losses, low, high, back_low, back_high, ahead_low, ahead_high, here, mine, theirs = outs

    @on_step(0)
    def _():
        total = swapped(place[0], jnp.sum(table[...], axis=0))
        losses[...] = stats[...] + jnp.log(total)
        for k in range(4):
            rows = slice(128 * k, 128 * k + 128)
            positive = jnp.where(marks(place, ids, k, 1)[0], 1.0, 0.0)
            grads[rows, :] = ((weights[rows, :] / total - positive) * inv_temp).astype(BF16)
        turned[...] = grads[...].T

    columns = jnp.concatenate([own[...], other[...]], axis=0)
    out = jnp.dot(grads[...], columns, preferred_element_type=F32)
    here[...] = out[0:128]
    halves = (back_low, back_high, ahead_low, ahead_high, low, high)
    for k, half in enumerate(halves):
        half[...] = out[128 + 64 * k : 192 + 64 * k].astype(half.dtype)
    rows = jnp.concatenate([p[...] for p in pool], axis=0)
    out = jnp.dot(turned[...], rows, preferred_element_type=F32)
    mine[...] = out[:128]
    theirs[...] = out[128:]


def total_body(here, back_low, back_high, ahead_low, ahead_high, total):
    half = back_low.shape[0]
    for rows, parts in (
        (slice(0, half), (back_low, ahead_low)),
        (slice(half, 2 * half), (back_high, ahead_high)),
    ):
        total[rows, :] = here[rows, :] + parts[0][...].astype(F32) + parts[1][...].astype(F32)


def on_device(queries, passages, positives, hard_negatives, thresholds):
    rows, width = queries.shape
    count = passages.shape[0]
    depth, breadth, ring = lax.axis_size(Z), lax.axis_size(X), lax.axis_size(Y)
    core, far, across, along = (lax.axis_index(a) for a in (CORE, Z, X, Y))
    half = count // 2
    plane = depth * breadth * rows
    total, pool, members = 2 * plane, ring * count, 2 * depth * breadth

    low, high = passages[:half], passages[half:]
    back_low, ahead_high = shifted(low, Y, 1), shifted(high, Y, -1)
    back_high, ahead_low = shifted(high, Y, 1), shifted(low, Y, -1)
    line = copies(queries, Z)
    line, back_low, ahead_high = lax.optimization_barrier((line, back_low, ahead_high))
    far_low, far_high = shifted(back_low, Y, 1), shifted(ahead_high, Y, -1)
    own = copies(line.reshape(depth * rows, width), X)

    def ordered(table):
        table = table.reshape(-1, depth, breadth, 2, rows)
        table = jnp.transpose(table, (0, 3, 2, 1, 4)).reshape(-1, 2, plane)
        return jnp.where(core == 0, table, jnp.flip(table, 1)).reshape(-1, total)

    ids = ordered(jnp.concatenate([positives[None, :], hard_negatives.T], axis=0))
    margin = ordered(jnp.broadcast_to(thresholds, (8, total)))
    steps = jnp.array([0, 1, 3, 2], jnp.int32)
    base = (((far * breadth + across) * 2 + core) * ring + (along - steps) % ring) * count
    place = jnp.concatenate([core.reshape(1), base]).astype(jnp.int32)
    own, far_low, far_high, back_high, ahead_low, ids, margin, place = lax.optimization_barrier(
        (own, far_low, far_high, back_high, ahead_low, ids, margin, place)
    )
    own = own.reshape(plane, width)
    other = shifted(own, CORE, 1)
    blocks = [passages, back_low, back_high, ahead_low, ahead_high, far_low, far_high]

    scores, table = call(
        score_body,
        [shape((pool, total), F32), shape((members, 2, total), F32)],
        [place, own, other, *blocks, ids],
        flops=2 * total * pool * width,
        scalars=1,
        tiled=range(1, 10),
    )
    table = lax.all_to_all(table, COL, 0, 0, tiled=True)
    weights, table, stats = call(
        soft_body,
        [shape((pool, total), F32), shape((members, 1, total), F32), shape((8, total), F32)],
        [place, table, margin, ids, scores],
        scalars=1,
    )
    table = lax.all_to_all(table, COL, 0, 0, tiled=True)
    piece, exact = shape((half, width), BF16), shape((half, width), F32)
    sums = [piece, piece, exact, piece, piece, exact] + [shape((count, width), F32)]
    losses, low, high, back_low, back_high, ahead_low, ahead_high, here, mine, theirs = call(
        grad_body,
        [shape((8, total), F32)] + sums + [shape((plane, width), F32)] * 2,
        [place, table, stats, ids, weights, own, other, *blocks],
        flops=4 * total * pool * width,
        scalars=1,
        tiled=(*range(5, 14), *range(15, 24)),
        scratch=[pltpu.VMEM((pool, total), BF16), pltpu.VMEM((total, pool), BF16)],
    )

    low, high = shifted(low, Y, -1), shifted(high, Y, 1)
    back_high, ahead_low = shifted(back_high, Y, -1), shifted(ahead_low, Y, 1)
    theirs = shifted(theirs, CORE, 1)
    back_low = shifted((back_low + low.astype(F32)).astype(BF16), Y, -1)
    ahead_high = shifted((ahead_high + high.astype(F32)).astype(BF16), Y, 1)
    grad_passages = call(
        total_body,
        [shape((count, width), F32)],
        [here, back_low, back_high, ahead_low, ahead_high],
        tiled=range(6),
    )[0]

    place_of = across * depth + far
    at = place_of * rows
    exact = lax.dynamic_slice_in_dim(mine, at, rows, 0) + lax.dynamic_slice_in_dim(theirs, at, rows, 0)
    sent = (mine + theirs).astype(BF16).reshape(breadth * depth, rows, width)
    parts = lax.all_to_all(sent, (X, Z), 0, 0, tiled=True)
    others = (lax.iota(jnp.int32, breadth * depth) != place_of)[:, None, None]
    grad_queries = exact + jnp.sum(jnp.where(others, parts.astype(F32), 0.0), axis=0)

    row_losses = lax.dynamic_slice_in_dim(losses[0], at, rows, 0)
    return row_losses, grad_queries, grad_passages


def solution(mesh):
    torus = Mesh(mesh.devices.reshape(mesh.shape[Y], 8, 4, 2), ROW_COL)
    in_specs = (P(ROW_COL, None), P(COL_ROW, None), P(Y), P(Y, None), P(Y))
    out_specs = (P(ROW_COL), P(ROW_COL, None), P(COL_ROW, None))
    return jax.shard_map(
        on_device, mesh=torus, in_specs=in_specs, out_specs=out_specs, check_vma=False
    )
```

```python
import functools

import jax
import jax.numpy as jnp
from jax import lax
from jax.experimental import pallas as pl
from jax.experimental.pallas import tpu as pltpu
from jax.sharding import Mesh
from jax.sharding import PartitionSpec as P

Y, Z, X, CORE = "row", "col_0", "col_1", "col_2"
COL = (Z, X, CORE)
ROW_COL = (Y, Z, X, CORE)
COL_ROW = (Z, X, CORE, Y)

inv_temp = 50.0
sharpness = 4.0
LOWEST = -3.0e38
F32, BF16 = jnp.float32, jnp.bfloat16
TILE = 1024


def shifted(value, axis, step):
    n = lax.axis_size(axis)
    return lax.ppermute(value, axis, [(i, (i + step) % n) for i in range(n)])


def copies(value, axis):
    n = lax.axis_size(axis)
    return lax.all_to_all(jnp.broadcast_to(value, (n, *value.shape)), axis, 0, 0, tiled=True)


def shape(dims, dtype):
    return jax.ShapeDtypeStruct(dims, dtype)


def call(body, outs, args, flops=0, scalars=0, tiled=(), scratch=(), outside=()):
    size = sum(a.size * a.dtype.itemsize for a in (*args, *outs))
    specs = []
    for k, a in enumerate((*args, *outs)):
        if k < scalars:
            specs.append(pl.BlockSpec(memory_space=pltpu.SMEM))
        elif k in tiled:
            specs.append(pl.BlockSpec((a.shape[0], TILE), lambda i: (0, i)))
        else:
            specs.append(pl.BlockSpec(a.shape, lambda i, n=len(a.shape): (0,) * n))
    kinds = [pltpu.HBM if k in outside else None for k in range(len(specs))]
    args = [
        a if kind is None else pltpu.with_memory_space_constraint(a, kind)
        for a, kind in zip(args, kinds)
    ]
    outs = [
        o if kind is None else pltpu.HBM(o.shape, o.dtype)
        for o, kind in zip(outs, kinds[len(args) :])
    ]
    steps = (*args, *outs)[tiled[0]].shape[1] // TILE if tiled else 1
    return pl.pallas_call(
        body,
        grid=(steps,),
        out_shape=outs,
        in_specs=specs[: len(args)],
        out_specs=specs[len(args) :],
        scratch_shapes=scratch,
        cost_estimate=pl.CostEstimate(flops=flops, bytes_accessed=size, transcendentals=0),
        compiler_params=pltpu.CompilerParams(vmem_limit_bytes=24 << 20),
    )(*args)


def swapped(core, row):
    half = row.shape[1] // 2
    return jnp.where(core == 0, row, jnp.concatenate([row[:, half:], row[:, :half]], axis=1))


def on_step(k):
    return pl.when(pl.program_id(0) == k)


def marks(place, ids, k, lines):
    column = place[1 + k] + lax.broadcasted_iota(jnp.int32, (128, ids.shape[1]), 0)
    found = [column == ids[slot : slot + 1, :] for slot in range(lines)]
    return found[0], functools.reduce(jnp.logical_or, found)


def score_body(place, own, other, *refs):
    pool, ids, scores, table = refs[:7], *refs[7:]

    @on_step(0)
    def _():
        scores[...] = jnp.zeros_like(scores)

    rows = jnp.concatenate([p[...] for p in pool], axis=0)
    columns = jnp.concatenate([own[...], other[...]], axis=0)
    scores[...] += lax.dot_general(
        rows, columns, (((1,), (1,)), ((), ())), preferred_element_type=F32
    )

    @pl.when(pl.program_id(0) == pl.num_programs(0) - 1)
    def _():
        tops = [[], []]
        for k in range(4):
            rows = slice(128 * k, 128 * k + 128)
            block = scores[rows, :] * inv_temp
            scores[rows, :] = block
            for top, mark in zip(tops, marks(place, ids, k, 8)):
                top.append(jnp.max(jnp.where(mark, block, LOWEST), axis=0, keepdims=True))
        lines = [swapped(place[0], functools.reduce(jnp.maximum, top)) for top in tops]
        table[...] = jnp.broadcast_to(jnp.concatenate(lines, axis=0)[None], table.shape)


def soft_body(place, table, margin_ref, ids, scores, weights, totals, stats):
    merged = swapped(place[0], jnp.max(table[...], axis=0))
    picked, kept = merged[0:1], merged[1:2]
    margin = margin_ref[0:1, :]
    ceiling = jnp.maximum(kept, picked + margin)
    sums = []
    for k in range(4):
        rows = slice(128 * k, 128 * k + 128)
        block = scores[rows, :]
        over = sharpness * (block - picked - margin)
        penalty = jnp.maximum(over, 0.0) + jnp.log(1.0 + jnp.exp(-jnp.abs(over)))
        logits = jnp.where(marks(place, ids, k, 8)[1], block, block - penalty)
        weight = jnp.exp(logits - ceiling)
        weights[rows, :] = weight
        sums.append(jnp.sum(weight, axis=0, keepdims=True))
    total = swapped(place[0], functools.reduce(jnp.add, sums))
    totals[...] = jnp.broadcast_to(total[None], totals.shape)
    stats[...] = jnp.broadcast_to(ceiling - picked, stats.shape)


def grad_body(place, table, stats, ids, weights, own, other, *refs):
    pool, outs, (grads, turned) = refs[:7], refs[7:17], refs[17:]
    losses, low, high, back_low, back_high, ahead_low, ahead_high, here, mine, theirs = outs

    @on_step(0)
    def _():
        total = swapped(place[0], jnp.sum(table[...], axis=0))
        losses[...] = stats[...] + jnp.log(total)
        for k in range(4):
            rows = slice(128 * k, 128 * k + 128)
            positive = jnp.where(marks(place, ids, k, 1)[0], 1.0, 0.0)
            grads[rows, :] = ((weights[rows, :] / total - positive) * inv_temp).astype(BF16)
        turned[...] = grads[...].T

    columns = jnp.concatenate([own[...], other[...]], axis=0)
    out = jnp.dot(grads[...], columns, preferred_element_type=F32)
    here[...] = out[0:128]
    halves = (back_low, back_high, ahead_low, ahead_high, low, high)
    for k, half in enumerate(halves):
        half[...] = out[128 + 64 * k : 192 + 64 * k].astype(half.dtype)
    rows = jnp.concatenate([p[...] for p in pool], axis=0)
    out = jnp.dot(turned[...], rows, preferred_element_type=F32)
    mine[...] = out[:128]
    theirs[...] = out[128:]


def total_body(here, back_low, back_high, ahead_low, ahead_high, total):
    half = back_low.shape[0]
    for rows, parts in (
        (slice(0, half), (back_low, ahead_low)),
        (slice(half, 2 * half), (back_high, ahead_high)),
    ):
        total[rows, :] = here[rows, :] + parts[0][...].astype(F32) + parts[1][...].astype(F32)


def on_device(queries, passages, positives, hard_negatives, thresholds):
    rows, width = queries.shape
    count = passages.shape[0]
    depth, breadth, ring = lax.axis_size(Z), lax.axis_size(X), lax.axis_size(Y)
    core, far, across, along = (lax.axis_index(a) for a in (CORE, Z, X, Y))
    half = count // 2
    plane = depth * breadth * rows
    total, pool, members = 2 * plane, ring * count, 2 * depth * breadth

    low, high = passages[:half], passages[half:]
    back_low, ahead_high = shifted(low, Y, 1), shifted(high, Y, -1)
    back_high, ahead_low = shifted(high, Y, 1), shifted(low, Y, -1)
    line = copies(queries, Z)
    line, back_low, ahead_high = lax.optimization_barrier((line, back_low, ahead_high))
    far_low, far_high = shifted(back_low, Y, 1), shifted(ahead_high, Y, -1)
    own = copies(line.reshape(depth * rows, width), X)

    def ordered(table):
        table = table.reshape(-1, depth, breadth, 2, rows)
        table = jnp.transpose(table, (0, 3, 2, 1, 4)).reshape(-1, 2, plane)
        return jnp.where(core == 0, table, jnp.flip(table, 1)).reshape(-1, total)

    ids = ordered(jnp.concatenate([positives[None, :], hard_negatives.T], axis=0))
    margin = ordered(jnp.broadcast_to(thresholds, (8, total)))
    steps = jnp.array([0, 1, 3, 2], jnp.int32)
    base = (((far * breadth + across) * 2 + core) * ring + (along - steps) % ring) * count
    place = jnp.concatenate([core.reshape(1), base]).astype(jnp.int32)
    own, far_low, far_high, back_high, ahead_low, ids, margin, place = lax.optimization_barrier(
        (own, far_low, far_high, back_high, ahead_low, ids, margin, place)
    )
    own = own.reshape(plane, width)
    other = shifted(own, CORE, 1)
    blocks = [passages, back_low, back_high, ahead_low, ahead_high, far_low, far_high]

    scores, table = call(
        score_body,
        [shape((pool, total), F32), shape((members, 2, total), F32)],
        [place, own, other, *blocks, ids],
        flops=2 * total * pool * width,
        scalars=1,
        tiled=range(1, 10),
    )
    table = lax.all_to_all(table, COL, 0, 0, tiled=True)
    weights, table, stats = call(
        soft_body,
        [shape((pool, total), F32), shape((members, 1, total), F32), shape((8, total), F32)],
        [place, table, margin, ids, scores],
        scalars=1,
    )
    table = lax.all_to_all(table, COL, 0, 0, tiled=True)
    piece, exact = shape((half, width), BF16), shape((half, width), F32)
    sums = [piece, piece, exact, piece, piece, exact] + [shape((count, width), F32)]
    losses, low, high, back_low, back_high, ahead_low, ahead_high, here, mine, theirs = call(
        grad_body,
        [shape((8, total), F32)] + sums + [shape((plane, width), F32)] * 2,
        [place, table, stats, ids, weights, own, other, *blocks],
        flops=4 * total * pool * width,
        scalars=1,
        tiled=(*range(5, 14), *range(15, 24)),
        scratch=[pltpu.VMEM((pool, total), BF16), pltpu.VMEM((total, pool), BF16)],
        outside=(15, 16, 17, 18, 19, 20, 21, 22, 23),
    )

    low, high = shifted(low, Y, -1), shifted(high, Y, 1)
    back_high, ahead_low = shifted(back_high, Y, -1), shifted(ahead_low, Y, 1)
    theirs = shifted(theirs, CORE, 1)
    back_low = shifted((back_low + low.astype(F32)).astype(BF16), Y, -1)
    ahead_high = shifted((ahead_high + high.astype(F32)).astype(BF16), Y, 1)

    place_of = across * depth + far
    at = place_of * rows
    exact = lax.dynamic_slice_in_dim(mine, at, rows, 0) + lax.dynamic_slice_in_dim(theirs, at, rows, 0)
    sent = (mine + theirs).astype(BF16).reshape(breadth * depth, rows, width)
    parts = lax.all_to_all(sent, (X, Z), 0, 0, tiled=True)
    others = (lax.iota(jnp.int32, breadth * depth) != place_of)[:, None, None]
    grad_queries = exact + jnp.sum(jnp.where(others, parts.astype(F32), 0.0), axis=0)

    grad_passages = call(
        total_body,
        [shape((count, width), F32)],
        [here, back_low, back_high, ahead_low, ahead_high],
        tiled=range(6),
    )[0]

    row_losses = lax.dynamic_slice_in_dim(losses[0], at, rows, 0)
    return row_losses, grad_queries, grad_passages


def solution(mesh):
    torus = Mesh(mesh.devices.reshape(mesh.shape[Y], 8, 4, 2), ROW_COL)
    in_specs = (P(ROW_COL, None), P(COL_ROW, None), P(Y), P(Y, None), P(Y))
    out_specs = (P(ROW_COL), P(ROW_COL, None), P(COL_ROW, None))
    return jax.shard_map(
        on_device, mesh=torus, in_specs=in_specs, out_specs=out_specs, check_vma=False
    )
```

```python
import functools

import jax
import jax.numpy as jnp
from jax import lax
from jax.experimental import pallas as pl
from jax.experimental.pallas import tpu as pltpu
from jax.sharding import Mesh
from jax.sharding import PartitionSpec as P

Y, Z, X, CORE = "row", "col_0", "col_1", "col_2"
COL = (Z, X, CORE)
ROW_COL = (Y, Z, X, CORE)
COL_ROW = (Z, X, CORE, Y)

inv_temp = 50.0
sharpness = 4.0
LOWEST = -3.0e38
F32, BF16 = jnp.float32, jnp.bfloat16
TILE = 1024


def shifted(value, axis, step):
    n = lax.axis_size(axis)
    return lax.ppermute(value, axis, [(i, (i + step) % n) for i in range(n)])


def copies(value, axis):
    n = lax.axis_size(axis)
    return lax.all_to_all(jnp.broadcast_to(value, (n, *value.shape)), axis, 0, 0, tiled=True)


def shape(dims, dtype):
    return jax.ShapeDtypeStruct(dims, dtype)


def call(body, outs, args, flops=0, scalars=0, tiled=(), scratch=(), outside=(), brief=False):
    size = sum(a.size * a.dtype.itemsize for a in (*args, *outs))
    specs = []
    for k, a in enumerate((*args, *outs)):
        if k < scalars:
            specs.append(pl.BlockSpec(memory_space=pltpu.SMEM))
        elif k in tiled:
            lead = (0,) * (len(a.shape) - 1)
            specs.append(pl.BlockSpec((*a.shape[:-1], TILE), lambda i, lead=lead: (*lead, i)))
        else:
            specs.append(pl.BlockSpec(a.shape, lambda i, n=len(a.shape): (0,) * n))
    kinds = [pltpu.HBM if k in outside else None for k in range(len(specs))]
    args = [
        a if kind is None else pltpu.with_memory_space_constraint(a, kind)
        for a, kind in zip(args, kinds)
    ]
    outs = [
        o if kind is None else pltpu.HBM(o.shape, o.dtype)
        for o, kind in zip(outs, kinds[len(args) :])
    ]
    steps = (*args, *outs)[tiled[0]].shape[-1] // TILE if tiled else 1
    return pl.pallas_call(
        body,
        grid=(steps,),
        out_shape=outs,
        in_specs=specs[: len(args)],
        out_specs=specs[len(args) :],
        scratch_shapes=scratch,
        cost_estimate=pl.CostEstimate(flops=flops, bytes_accessed=1024 if brief else size, transcendentals=0),
        compiler_params=pltpu.CompilerParams(vmem_limit_bytes=24 << 20),
    )(*args)


def on_step(k):
    return pl.when(pl.program_id(0) == k)


def marks(place, ids, block, lines):
    column = place[block] + lax.broadcasted_iota(jnp.int32, (128, ids.shape[1]), 0)
    found = [column == ids[slot : slot + 1, :] for slot in range(lines)]
    return found[0], functools.reduce(jnp.logical_or, found)


BLOCKS = [
    (4 * m + k, slice(384 * m + 128 * k, 384 * m + 128 * k + 128) if k < 3 else None, slice(128 * m, 128 * m + 128))
    for m in range(2)
    for k in range(4)
]


def products(own, pool, scores):
    @on_step(0)
    def _():
        scores[...] = jnp.zeros_like(scores)

    rows = jnp.concatenate([p[...] for p in pool], axis=0)
    scores[...] += lax.dot_general(
        rows, own[...], (((1,), (1,)), ((), ())), preferred_element_type=F32
    )


def near_body(own, *refs):
    products(own, refs[:-1], refs[-1])


def far_body(place, own, *refs):
    pool, near, ids, far, table = refs[:4], *refs[4:]
    products(own, pool, far)

    @pl.when(pl.program_id(0) == pl.num_programs(0) - 1)
    def _():
        tops = [[], []]
        for block, at, other in BLOCKS:
            value = (far[other, :] if at is None else near[at, :]) * inv_temp
            for top, mark in zip(tops, marks(place, ids, block, 8)):
                top.append(jnp.max(jnp.where(mark, value, LOWEST), axis=0, keepdims=True))
        lines = [functools.reduce(jnp.maximum, top) for top in tops]
        table[...] = jnp.broadcast_to(jnp.concatenate(lines, axis=0)[None], table.shape)


def soft_body(place, table, margin_ref, ids, near, far, weights, totals, stats):
    merged = jnp.max(table[...], axis=0)
    picked, kept = merged[0:1], merged[1:2]
    margin = margin_ref[0:1, :]
    ceiling = jnp.maximum(kept, picked + margin)
    sums = []
    for block, at, other in BLOCKS:
        value = (far[other, :] if at is None else near[at, :]) * inv_temp
        over = sharpness * (value - picked - margin)
        penalty = jnp.maximum(over, 0.0) + jnp.log(1.0 + jnp.exp(-jnp.abs(over)))
        logits = jnp.where(marks(place, ids, block, 8)[1], value, value - penalty)
        weight = jnp.exp(logits - ceiling)
        weights[128 * block : 128 * block + 128, :] = weight
        sums.append(jnp.sum(weight, axis=0, keepdims=True))
    totals[...] = jnp.broadcast_to(functools.reduce(jnp.add, sums)[None], totals.shape)
    stats[...] = jnp.broadcast_to(ceiling - picked, stats.shape)


def grad_body(place, table, stats, ids, weights, losses, mine, theirs):
    total = jnp.sum(table[...], axis=0)
    losses[...] = stats[...] + jnp.log(total)
    for block in range(8):
        positive = jnp.where(marks(place, ids, block, 1)[0], 1.0, 0.0)
        rows = slice(128 * block, 128 * block + 128)
        value = ((weights[rows, :] / total - positive) * inv_temp).astype(BF16)
        rows = slice(128 * (block % 4), 128 * (block % 4) + 128)
        (mine if block < 4 else theirs)[rows, :] = value


def query_body(place, mine, theirs, *refs):
    pool, sent, exact, turned, sums = refs[:14], *refs[14:]

    @on_step(0)
    def _():
        turned[...] = jnp.concatenate([mine[...], theirs[...]], axis=0).T

    rows = jnp.concatenate([p[...] for p in pool], axis=0)
    sums[...] = jnp.dot(turned[...], rows, preferred_element_type=F32)
    sent[...] = sums[...].reshape(sent.shape).astype(BF16)
    exact[...] = sums[pl.ds(pl.multiple_of(place[8], 8), 8), :]


def passage_body(mine, arrived, own, other, down, up, low, high, here):
    weights = jnp.concatenate([mine[...], arrived[...]], axis=1)
    columns = jnp.concatenate([own[...], other[...]], axis=0)
    out = jnp.dot(weights, columns, preferred_element_type=F32)
    here[...] = out[0:128]
    low[...] = out[128:192]
    high[...] = out[320:384]
    down[0:64, :] = out[384:448].astype(BF16)
    down[64:128, :] = out[192:256].astype(BF16)
    up[0:64, :] = out[256:320].astype(BF16)
    up[64:128, :] = out[448:512].astype(BF16)


def total_body(here, down, up, low, high, total):
    total[0:64, :] = here[0:64, :] + up[0:64, :].astype(F32) + low[...].astype(F32)
    total[64:128, :] = here[64:128, :] + down[64:128, :].astype(F32) + high[...].astype(F32)


def on_device(queries, passages, positives, hard_negatives, thresholds):
    rows, width = queries.shape
    count = passages.shape[0]
    depth, breadth, ring = lax.axis_size(Z), lax.axis_size(X), lax.axis_size(Y)
    core, far, across, along = (lax.axis_index(a) for a in (CORE, Z, X, Y))
    half, members = count // 2, depth * breadth
    plane, pool = members * rows, ring * count

    low, high = passages[:half], passages[half:]
    back_low, ahead_high = shifted(low, Y, 1), shifted(high, Y, -1)
    back_high, ahead_low = shifted(high, Y, 1), shifted(low, Y, -1)
    line = copies(queries, Z)
    line, back_low, ahead_high = lax.optimization_barrier((line, back_low, ahead_high))
    far_low, far_high = shifted(back_low, Y, 1), shifted(ahead_high, Y, -1)
    own = copies(line.reshape(depth * rows, width), X)

    def ordered(table):
        table = table.reshape(-1, depth, breadth, 2, rows)
        table = lax.dynamic_index_in_dim(table, core, 3, keepdims=False)
        return jnp.swapaxes(table, 1, 2).reshape(-1, plane)

    ids = ordered(jnp.concatenate([positives[None, :], hard_negatives.T], axis=0))
    margin = ordered(jnp.broadcast_to(thresholds, (8, thresholds.shape[0])))
    steps = jnp.array([0, 1, 3, 2], jnp.int32)
    cores = jnp.stack([core, 1 - core])[:, None]
    base = (((far * breadth + across) * 2 + cores) * ring + (along - steps) % ring) * count
    place_of = across * depth + far
    at = place_of * rows
    place = jnp.concatenate([base.reshape(-1), (at // 8 * 8).reshape(1)]).astype(jnp.int32)

    near = [passages, back_low, back_high, ahead_low, ahead_high]
    near_pair = [shifted(p, CORE, 1) for p in near]
    own, near, near_pair, ids, margin, place = lax.optimization_barrier(
        (own, near, near_pair, ids, margin, place)
    )
    own = own.reshape(plane, width)
    other = shifted(own, CORE, 1)
    far_pair = [shifted(far_low, CORE, 1), shifted(far_high, CORE, 1)]

    near_scores = call(
        near_body,
        [shape((6 * count, plane), F32)],
        [own, *near, *near_pair],
        flops=2 * plane * 6 * count * width,
        tiled=range(11),
    )[0]
    far_scores, table = call(
        far_body,
        [shape((2 * count, plane), F32), shape((members, 2, plane), F32)],
        [place, own, far_low, far_high, *far_pair, near_scores, ids],
        flops=2 * plane * 2 * count * width,
        scalars=1,
        tiled=range(1, 6),
        outside=(8, 9),
    )
    table = lax.all_to_all(table, (Z, X), 0, 0, tiled=True)
    weights, table, stats = call(
        soft_body,
        [shape((2 * pool, plane), F32), shape((members, 1, plane), F32), shape((8, plane), F32)],
        [place, table, margin, ids, near_scores, far_scores],
        scalars=1,
    )
    table = lax.all_to_all(table, (Z, X), 0, 0, tiled=True)
    losses, mine, theirs = call(
        grad_body,
        [shape((8, plane), F32)] + [shape((pool, plane), BF16)] * 2,
        [place, table, stats, ids, weights],
        scalars=1,
    )
    arrived = shifted(theirs, CORE, 1)

    sent, exact = call(
        query_body,
        [shape((members, rows, width), BF16), shape((8, width), F32)],
        [place, mine, theirs, *near, far_low, far_high, *near_pair, *far_pair],
        scalars=1,
        tiled=range(3, 19),
        scratch=[pltpu.VMEM((plane, 2 * pool), BF16), pltpu.VMEM((plane, TILE), F32)],
        outside=(17, 18),
        brief=True,
    )
    parts = lax.all_to_all(sent, (X, Z), 0, 0, tiled=True)
    exact = lax.dynamic_slice_in_dim(exact, at % 8, rows, 0)
    others = (lax.iota(jnp.int32, members) != place_of)[:, None, None]
    grad_queries = exact + jnp.sum(jnp.where(others, parts.astype(F32), 0.0), axis=0)

    block = [shape((count, width), BF16)] * 2 + [shape((half, width), F32)] * 2
    down, up, low, high, here = call(
        passage_body,
        block + [shape((count, width), F32)],
        [mine, arrived, own, other],
        flops=4 * plane * pool * width,
        tiled=range(2, 9),
        outside=range(4, 9),
    )
    down, up = shifted(down, Y, -1), shifted(up, Y, 1)
    down, up = lax.optimization_barrier((down, up))
    low = shifted((low + down[:half].astype(F32)).astype(BF16), Y, -1)
    high = shifted((high + up[half:].astype(F32)).astype(BF16), Y, 1)
    grad_passages = call(
        total_body, [shape((count, width), F32)], [here, down, up, low, high], tiled=range(6), outside=(0, 3, 4)
    )[0]

    row_losses = lax.dynamic_slice_in_dim(losses[0], at, rows, 0)
    return row_losses, grad_queries, grad_passages


def solution(mesh):
    torus = Mesh(mesh.devices.reshape(mesh.shape[Y], 8, 4, 2), ROW_COL)
    in_specs = (P(ROW_COL, None), P(COL_ROW, None), P(Y), P(Y, None), P(Y))
    out_specs = (P(ROW_COL), P(ROW_COL, None), P(COL_ROW, None))
    return jax.shard_map(
        on_device, mesh=torus, in_specs=in_specs, out_specs=out_specs, check_vma=False
    )
```

```python
import functools

import jax
import jax.numpy as jnp
from jax import lax
from jax.experimental import pallas as pl
from jax.experimental.pallas import tpu as pltpu
from jax.sharding import Mesh
from jax.sharding import PartitionSpec as P

Y, Z, X, CORE = "row", "col_0", "col_1", "col_2"
COL = (Z, X, CORE)
ROW_COL = (Y, Z, X, CORE)
COL_ROW = (Z, X, CORE, Y)

inv_temp = 50.0
sharpness = 4.0
LOWEST = -3.0e38
F32, BF16 = jnp.float32, jnp.bfloat16
TILE = 1024


def shifted(value, axis, step):
    n = lax.axis_size(axis)
    return lax.ppermute(value, axis, [(i, (i + step) % n) for i in range(n)])


def copies(value, axis):
    n = lax.axis_size(axis)
    return lax.all_to_all(jnp.broadcast_to(value, (n, *value.shape)), axis, 0, 0, tiled=True)


def shape(dims, dtype):
    return jax.ShapeDtypeStruct(dims, dtype)


def call(body, outs, args, flops=0, scalars=0, tiled=(), scratch=(), outside=()):
    size = sum(a.size * a.dtype.itemsize for a in (*args, *outs))
    specs = []
    for k, a in enumerate((*args, *outs)):
        if k < scalars:
            specs.append(pl.BlockSpec(memory_space=pltpu.SMEM))
        elif k in tiled:
            lead = (0,) * (len(a.shape) - 1)
            specs.append(pl.BlockSpec((*a.shape[:-1], TILE), lambda i, lead=lead: (*lead, i)))
        else:
            specs.append(pl.BlockSpec(a.shape, lambda i, n=len(a.shape): (0,) * n))
    kinds = [pltpu.HBM if k in outside else None for k in range(len(specs))]
    args = [
        a if kind is None else pltpu.with_memory_space_constraint(a, kind)
        for a, kind in zip(args, kinds)
    ]
    outs = [
        o if kind is None else pltpu.HBM(o.shape, o.dtype)
        for o, kind in zip(outs, kinds[len(args) :])
    ]
    steps = (*args, *outs)[tiled[0]].shape[-1] // TILE if tiled else 1
    return pl.pallas_call(
        body,
        grid=(steps,),
        out_shape=outs,
        in_specs=specs[: len(args)],
        out_specs=specs[len(args) :],
        scratch_shapes=scratch,
        cost_estimate=pl.CostEstimate(flops=flops, bytes_accessed=size, transcendentals=0),
        compiler_params=pltpu.CompilerParams(vmem_limit_bytes=24 << 20),
    )(*args)


def swapped(core, row):
    half = row.shape[1] // 2
    return jnp.where(core == 0, row, jnp.concatenate([row[:, half:], row[:, :half]], axis=1))


def on_step(k):
    return pl.when(pl.program_id(0) == k)


def marks(place, ids, k, lines):
    column = place[1 + k] + lax.broadcasted_iota(jnp.int32, (128, ids.shape[1]), 0)
    found = [column == ids[slot : slot + 1, :] for slot in range(lines)]
    return found[0], functools.reduce(jnp.logical_or, found)


def score_body(place, own, other, *refs):
    pool, ids, scores, table = refs[:7], *refs[7:]

    @on_step(0)
    def _():
        scores[...] = jnp.zeros_like(scores)

    rows = jnp.concatenate([p[...] for p in pool], axis=0)
    columns = jnp.concatenate([own[...], other[...]], axis=0)
    scores[...] += lax.dot_general(
        rows, columns, (((1,), (1,)), ((), ())), preferred_element_type=F32
    )

    @pl.when(pl.program_id(0) == pl.num_programs(0) - 1)
    def _():
        tops = [[], []]
        for k in range(4):
            rows = slice(128 * k, 128 * k + 128)
            block = scores[rows, :] * inv_temp
            scores[rows, :] = block
            for top, mark in zip(tops, marks(place, ids, k, 8)):
                top.append(jnp.max(jnp.where(mark, block, LOWEST), axis=0, keepdims=True))
        lines = [swapped(place[0], functools.reduce(jnp.maximum, top)) for top in tops]
        table[...] = jnp.broadcast_to(jnp.concatenate(lines, axis=0)[None], table.shape)


def soft_body(place, table, margin_ref, ids, scores, weights, totals, stats):
    merged = swapped(place[0], jnp.max(table[...], axis=0))
    picked, kept = merged[0:1], merged[1:2]
    margin = margin_ref[0:1, :]
    ceiling = jnp.maximum(kept, picked + margin)
    sums = []
    for k in range(4):
        rows = slice(128 * k, 128 * k + 128)
        block = scores[rows, :]
        over = sharpness * (block - picked - margin)
        penalty = jnp.maximum(over, 0.0) + jnp.log(1.0 + jnp.exp(-jnp.abs(over)))
        logits = jnp.where(marks(place, ids, k, 8)[1], block, block - penalty)
        weight = jnp.exp(logits - ceiling)
        weights[rows, :] = weight
        sums.append(jnp.sum(weight, axis=0, keepdims=True))
    total = swapped(place[0], functools.reduce(jnp.add, sums))
    totals[...] = jnp.broadcast_to(total[None], totals.shape)
    stats[...] = jnp.broadcast_to(ceiling - picked, stats.shape)


def grad_body(place, table, stats, ids, weights, own, other, *refs):
    pool, outs, (grads, turned) = refs[:7], refs[7:17], refs[17:]
    losses, low, high, back_low, back_high, ahead_low, ahead_high, here, mine, theirs = outs

    @on_step(0)
    def _():
        total = swapped(place[0], jnp.sum(table[...], axis=0))
        losses[...] = stats[...] + jnp.log(total)
        for k in range(4):
            rows = slice(128 * k, 128 * k + 128)
            positive = jnp.where(marks(place, ids, k, 1)[0], 1.0, 0.0)
            grads[rows, :] = ((weights[rows, :] / total - positive) * inv_temp).astype(BF16)
        turned[...] = grads[...].T

    columns = jnp.concatenate([own[...], other[...]], axis=0)
    out = jnp.dot(grads[...], columns, preferred_element_type=F32)
    here[...] = out[0:128]
    halves = (back_low, back_high, ahead_low, ahead_high, low, high)
    for k, half in enumerate(halves):
        half[...] = out[128 + 64 * k : 192 + 64 * k].astype(half.dtype)
    rows = jnp.concatenate([p[...] for p in pool], axis=0)
    out = jnp.dot(turned[...], rows, preferred_element_type=F32)
    mine[...] = out[:128]
    theirs[...] = out[128:]


def join_body(place, mine, theirs, sent, exact, sums):
    sums[...] = mine[...] + theirs[...]
    sent[...] = sums[...].reshape(sent.shape).astype(BF16)
    exact[...] = sums[pl.ds(pl.multiple_of(place[5], 8), 8), :]


def total_body(here, back_low, back_high, ahead_low, ahead_high, total):
    half = back_low.shape[0]
    for rows, parts in (
        (slice(0, half), (back_low, ahead_low)),
        (slice(half, 2 * half), (back_high, ahead_high)),
    ):
        total[rows, :] = here[rows, :] + parts[0][...].astype(F32) + parts[1][...].astype(F32)


def on_device(queries, passages, positives, hard_negatives, thresholds):
    rows, width = queries.shape
    count = passages.shape[0]
    depth, breadth, ring = lax.axis_size(Z), lax.axis_size(X), lax.axis_size(Y)
    core, far, across, along = (lax.axis_index(a) for a in (CORE, Z, X, Y))
    half = count // 2
    plane = depth * breadth * rows
    total, pool, members = 2 * plane, ring * count, 2 * depth * breadth

    low, high = passages[:half], passages[half:]
    back_low, ahead_high = shifted(low, Y, 1), shifted(high, Y, -1)
    back_high, ahead_low = shifted(high, Y, 1), shifted(low, Y, -1)
    line = copies(queries, Z)
    line, back_low, ahead_high = lax.optimization_barrier((line, back_low, ahead_high))
    far_low, far_high = shifted(back_low, Y, 1), shifted(ahead_high, Y, -1)
    own = copies(line.reshape(depth * rows, width), X)

    def ordered(table):
        table = table.reshape(-1, depth, breadth, 2, rows)
        table = jnp.transpose(table, (0, 3, 2, 1, 4)).reshape(-1, 2, plane)
        return jnp.where(core == 0, table, jnp.flip(table, 1)).reshape(-1, total)

    ids = ordered(jnp.concatenate([positives[None, :], hard_negatives.T], axis=0))
    margin = ordered(jnp.broadcast_to(thresholds, (8, total)))
    steps = jnp.array([0, 1, 3, 2], jnp.int32)
    base = (((far * breadth + across) * 2 + core) * ring + (along - steps) % ring) * count
    place_of = across * depth + far
    at = place_of * rows
    place = jnp.concatenate([core.reshape(1), base, (at // 8 * 8).reshape(1)]).astype(jnp.int32)
    own, far_low, far_high, back_high, ahead_low, ids, margin, place = lax.optimization_barrier(
        (own, far_low, far_high, back_high, ahead_low, ids, margin, place)
    )
    own = own.reshape(plane, width)
    other = shifted(own, CORE, 1)
    blocks = [passages, back_low, back_high, ahead_low, ahead_high, far_low, far_high]

    scores, table = call(
        score_body,
        [shape((pool, total), F32), shape((members, 2, total), F32)],
        [place, own, other, *blocks, ids],
        flops=2 * total * pool * width,
        scalars=1,
        tiled=range(1, 10),
    )
    table = lax.all_to_all(table, COL, 0, 0, tiled=True)
    weights, table, stats = call(
        soft_body,
        [shape((pool, total), F32), shape((members, 1, total), F32), shape((8, total), F32)],
        [place, table, margin, ids, scores],
        scalars=1,
    )
    table = lax.all_to_all(table, COL, 0, 0, tiled=True)
    piece, exact = shape((half, width), BF16), shape((half, width), F32)
    sums = [piece, piece, exact, piece, piece, exact] + [shape((count, width), F32)]
    losses, low, high, back_low, back_high, ahead_low, ahead_high, here, mine, theirs = call(
        grad_body,
        [shape((8, total), F32)] + sums + [shape((plane, width), F32)] * 2,
        [place, table, stats, ids, weights, own, other, *blocks],
        flops=4 * total * pool * width,
        scalars=1,
        tiled=(*range(5, 14), *range(15, 24)),
        scratch=[pltpu.VMEM((pool, total), BF16), pltpu.VMEM((total, pool), BF16)],
        outside=(15, 16, 17, 18, 19, 20, 21, 22, 23),
    )

    low, high = shifted(low, Y, -1), shifted(high, Y, 1)
    back_high, ahead_low = shifted(back_high, Y, -1), shifted(ahead_low, Y, 1)
    theirs = shifted(theirs, CORE, 1)
    back_low = shifted((back_low + low.astype(F32)).astype(BF16), Y, -1)
    ahead_high = shifted((ahead_high + high.astype(F32)).astype(BF16), Y, 1)

    sent, exact = call(
        join_body,
        [shape((breadth * depth, rows, width), BF16), shape((8, width), F32)],
        [place, mine, theirs],
        scalars=1,
        tiled=(1, 2, 3, 4),
        scratch=[pltpu.VMEM((plane, TILE), F32)],
        outside=(1, 3, 4),
    )
    exact = lax.dynamic_slice_in_dim(exact, at % 8, rows, 0)
    parts = lax.all_to_all(sent, (X, Z), 0, 0, tiled=True)
    others = (lax.iota(jnp.int32, breadth * depth) != place_of)[:, None, None]
    grad_queries = exact + jnp.sum(jnp.where(others, parts.astype(F32), 0.0), axis=0)

    sent, exact = call(
        join_body,
        [shape((breadth * depth, rows, width), BF16), shape((8, width), F32)],
        [place, mine, theirs],
        scalars=1,
        tiled=(1, 2, 3, 4),
        scratch=[pltpu.VMEM((plane, TILE), F32)],
        outside=(1, 3, 4),
    )
    exact = lax.dynamic_slice_in_dim(exact, at % 8, rows, 0)
    parts = lax.all_to_all(sent, (X, Z), 0, 0, tiled=True)
    others = (lax.iota(jnp.int32, breadth * depth) != place_of)[:, None, None]
    grad_queries = exact + jnp.sum(jnp.where(others, parts.astype(F32), 0.0), axis=0)

    grad_passages = call(
        total_body,
        [shape((count, width), F32)],
        [here, back_low, back_high, ahead_low, ahead_high],
        tiled=range(6),
    )[0]

    row_losses = lax.dynamic_slice_in_dim(losses[0], at, rows, 0)
    return row_losses, grad_queries, grad_passages


def solution(mesh):
    torus = Mesh(mesh.devices.reshape(mesh.shape[Y], 8, 4, 2), ROW_COL)
    in_specs = (P(ROW_COL, None), P(COL_ROW, None), P(Y), P(Y, None), P(Y))
    out_specs = (P(ROW_COL), P(ROW_COL, None), P(COL_ROW, None))
    return jax.shard_map(
        on_device, mesh=torus, in_specs=in_specs, out_specs=out_specs, check_vma=False
    )
```

```python
import functools

import jax
import jax.numpy as jnp
from jax import lax
from jax.experimental import pallas as pl
from jax.experimental.pallas import tpu as pltpu
from jax.sharding import Mesh
from jax.sharding import PartitionSpec as P

Y, Z, X, CORE = "row", "col_0", "col_1", "col_2"
COL = (Z, X, CORE)
ROW_COL = (Y, Z, X, CORE)
COL_ROW = (Z, X, CORE, Y)

inv_temp = 50.0
sharpness = 4.0
LOWEST = -3.0e38
F32, BF16 = jnp.float32, jnp.bfloat16
TILE = 1024


def shifted(value, axis, step):
    n = lax.axis_size(axis)
    return lax.ppermute(value, axis, [(i, (i + step) % n) for i in range(n)])


def copies(value, axis):
    n = lax.axis_size(axis)
    return lax.all_to_all(jnp.broadcast_to(value, (n, *value.shape)), axis, 0, 0, tiled=True)


def shape(dims, dtype):
    return jax.ShapeDtypeStruct(dims, dtype)


def call(body, outs, args, flops=0, scalars=0, tiled=(), scratch=(), outside=()):
    size = sum(a.size * a.dtype.itemsize for a in (*args, *outs))
    specs = []
    for k, a in enumerate((*args, *outs)):
        if k < scalars:
            specs.append(pl.BlockSpec(memory_space=pltpu.SMEM))
        elif k in tiled:
            specs.append(pl.BlockSpec((a.shape[0], TILE), lambda i: (0, i)))
        else:
            specs.append(pl.BlockSpec(a.shape, lambda i, n=len(a.shape): (0,) * n))
    kinds = [pltpu.HBM if k in outside else None for k in range(len(specs))]
    args = [
        a if kind is None else pltpu.with_memory_space_constraint(a, kind)
        for a, kind in zip(args, kinds)
    ]
    outs = [
        o if kind is None else pltpu.HBM(o.shape, o.dtype)
        for o, kind in zip(outs, kinds[len(args) :])
    ]
    steps = (*args, *outs)[tiled[0]].shape[1] // TILE if tiled else 1
    return pl.pallas_call(
        body,
        grid=(steps,),
        out_shape=outs,
        in_specs=specs[: len(args)],
        out_specs=specs[len(args) :],
        scratch_shapes=scratch,
        cost_estimate=pl.CostEstimate(flops=flops, bytes_accessed=size, transcendentals=0),
        compiler_params=pltpu.CompilerParams(vmem_limit_bytes=(24 if flops else 8) << 20),
    )(*args)


def swapped(core, row):
    half = row.shape[1] // 2
    return jnp.where(core == 0, row, jnp.concatenate([row[:, half:], row[:, :half]], axis=1))


def on_step(k):
    return pl.when(pl.program_id(0) == k)


def marks(place, ids, k, lines):
    column = place[1 + k] + lax.broadcasted_iota(jnp.int32, (128, ids.shape[1]), 0)
    found = [column == ids[slot : slot + 1, :] for slot in range(lines)]
    return found[0], functools.reduce(jnp.logical_or, found)


def score_body(place, own, other, *refs):
    pool, ids, scores, table = refs[:7], *refs[7:]

    @on_step(0)
    def _():
        scores[...] = jnp.zeros_like(scores)

    rows = jnp.concatenate([p[...] for p in pool], axis=0)
    columns = jnp.concatenate([own[...], other[...]], axis=0)
    scores[...] += lax.dot_general(
        rows, columns, (((1,), (1,)), ((), ())), preferred_element_type=F32
    )

    @pl.when(pl.program_id(0) == pl.num_programs(0) - 1)
    def _():
        tops = [[], []]
        for k in range(4):
            rows = slice(128 * k, 128 * k + 128)
            block = scores[rows, :] * inv_temp
            scores[rows, :] = block
            for top, mark in zip(tops, marks(place, ids, k, 8)):
                top.append(jnp.max(jnp.where(mark, block, LOWEST), axis=0, keepdims=True))
        lines = [swapped(place[0], functools.reduce(jnp.maximum, top)) for top in tops]
        table[...] = jnp.broadcast_to(jnp.concatenate(lines, axis=0)[None], table.shape)


def soft_body(place, table, margin_ref, ids, scores, weights, totals, stats):
    merged = swapped(place[0], jnp.max(table[...], axis=0))
    picked, kept = merged[0:1], merged[1:2]
    margin = margin_ref[0:1, :]
    ceiling = jnp.maximum(kept, picked + margin)
    sums = []
    for k in range(4):
        rows = slice(128 * k, 128 * k + 128)
        block = scores[rows, :]
        over = sharpness * (block - picked - margin)
        penalty = jnp.maximum(over, 0.0) + jnp.log(1.0 + jnp.exp(-jnp.abs(over)))
        logits = jnp.where(marks(place, ids, k, 8)[1], block, block - penalty)
        weight = jnp.exp(logits - ceiling)
        weights[rows, :] = weight
        sums.append(jnp.sum(weight, axis=0, keepdims=True))
    total = swapped(place[0], functools.reduce(jnp.add, sums))
    totals[...] = jnp.broadcast_to(total[None], totals.shape)
    stats[...] = jnp.broadcast_to(ceiling - picked, stats.shape)


def grad_body(place, table, stats, ids, weights, own, other, *refs):
    pool, outs, (grads, turned) = refs[:7], refs[7:17], refs[17:]
    losses, low, high, back_low, back_high, ahead_low, ahead_high, here, mine, theirs = outs

    @on_step(0)
    def _():
        total = swapped(place[0], jnp.sum(table[...], axis=0))
        losses[...] = stats[...] + jnp.log(total)
        for k in range(4):
            rows = slice(128 * k, 128 * k + 128)
            positive = jnp.where(marks(place, ids, k, 1)[0], 1.0, 0.0)
            grads[rows, :] = ((weights[rows, :] / total - positive) * inv_temp).astype(BF16)
        turned[...] = grads[...].T

    columns = jnp.concatenate([own[...], other[...]], axis=0)
    out = jnp.dot(grads[...], columns, preferred_element_type=F32)
    here[...] = out[0:128]
    halves = (back_low, back_high, ahead_low, ahead_high, low, high)
    for k, half in enumerate(halves):
        half[...] = out[128 + 64 * k : 192 + 64 * k].astype(half.dtype)
    rows = jnp.concatenate([p[...] for p in pool], axis=0)
    out = jnp.dot(turned[...], rows, preferred_element_type=F32)
    mine[...] = out[:128]
    theirs[...] = out[128:]


def total_body(here, back_low, back_high, ahead_low, ahead_high, total):
    half = back_low.shape[0]
    for rows, parts in (
        (slice(0, half), (back_low, ahead_low)),
        (slice(half, 2 * half), (back_high, ahead_high)),
    ):
        total[rows, :] = here[rows, :] + parts[0][...].astype(F32) + parts[1][...].astype(F32)


def on_device(queries, passages, positives, hard_negatives, thresholds):
    rows, width = queries.shape
    count = passages.shape[0]
    depth, breadth, ring = lax.axis_size(Z), lax.axis_size(X), lax.axis_size(Y)
    core, far, across, along = (lax.axis_index(a) for a in (CORE, Z, X, Y))
    half = count // 2
    plane = depth * breadth * rows
    total, pool, members = 2 * plane, ring * count, 2 * depth * breadth

    low, high = passages[:half], passages[half:]
    back_low, ahead_high = shifted(low, Y, 1), shifted(high, Y, -1)
    back_high, ahead_low = shifted(high, Y, 1), shifted(low, Y, -1)
    line = copies(queries, Z)
    line, back_low, ahead_high = lax.optimization_barrier((line, back_low, ahead_high))
    far_low, far_high = shifted(back_low, Y, 1), shifted(ahead_high, Y, -1)
    own = copies(line.reshape(depth * rows, width), X)

    def ordered(table):
        table = table.reshape(-1, depth, breadth, 2, rows)
        table = jnp.transpose(table, (0, 3, 2, 1, 4)).reshape(-1, 2, plane)
        return jnp.where(core == 0, table, jnp.flip(table, 1)).reshape(-1, total)

    ids = ordered(jnp.concatenate([positives[None, :], hard_negatives.T], axis=0))
    margin = ordered(jnp.broadcast_to(thresholds, (8, total)))
    steps = jnp.array([0, 1, 3, 2], jnp.int32)
    base = (((far * breadth + across) * 2 + core) * ring + (along - steps) % ring) * count
    place = jnp.concatenate([core.reshape(1), base]).astype(jnp.int32)
    own, far_low, far_high, back_high, ahead_low, ids, margin, place = lax.optimization_barrier(
        (own, far_low, far_high, back_high, ahead_low, ids, margin, place)
    )
    own = own.reshape(plane, width)
    other = shifted(own, CORE, 1)
    blocks = [passages, back_low, back_high, ahead_low, ahead_high, far_low, far_high]

    scores, table = call(
        score_body,
        [shape((pool, total), F32), shape((members, 2, total), F32)],
        [place, own, other, *blocks, ids],
        flops=2 * total * pool * width,
        scalars=1,
        tiled=range(1, 10),
    )
    table = lax.all_to_all(table, COL, 0, 0, tiled=True)
    weights, table, stats = call(
        soft_body,
        [shape((pool, total), F32), shape((members, 1, total), F32), shape((8, total), F32)],
        [place, table, margin, ids, scores],
        scalars=1,
    )
    table = lax.all_to_all(table, COL, 0, 0, tiled=True)
    sums = [shape((half, width), BF16)] * 6 + [shape((count, width), F32)]
    losses, low, high, back_low, back_high, ahead_low, ahead_high, here, mine, theirs = call(
        grad_body,
        [shape((8, total), F32)] + sums + [shape((plane, width), F32)] * 2,
        [place, table, stats, ids, weights, own, other, *blocks],
        flops=4 * total * pool * width,
        scalars=1,
        tiled=(*range(5, 14), *range(15, 24)),
        scratch=[pltpu.VMEM((pool, total), BF16), pltpu.VMEM((total, pool), BF16)],
        outside=(15, 16, 17, 18, 19, 20, 21, 22, 23),
    )

    low, high = shifted(low, Y, -1), shifted(high, Y, 1)
    back_high, ahead_low = shifted(back_high, Y, -1), shifted(ahead_low, Y, 1)
    theirs = shifted(theirs, CORE, 1)
    back_low = shifted((back_low.astype(F32) + low.astype(F32)).astype(BF16), Y, -1)
    ahead_high = shifted((ahead_high.astype(F32) + high.astype(F32)).astype(BF16), Y, 1)

    place_of = across * depth + far
    at = place_of * rows
    exact = lax.dynamic_slice_in_dim(mine, at, rows, 0) + lax.dynamic_slice_in_dim(theirs, at, rows, 0)
    sent = (mine + theirs).astype(BF16).reshape(breadth * depth, rows, width)
    exact, sent = lax.optimization_barrier((exact, sent))
    parts = lax.all_to_all(sent, (X, Z), 0, 0, tiled=True)
    others = (lax.iota(jnp.int32, breadth * depth) != place_of)[:, None, None]
    grad_queries = exact + jnp.sum(jnp.where(others, parts.astype(F32), 0.0), axis=0)

    grad_passages = call(
        total_body,
        [shape((count, width), F32)],
        [here, back_low, back_high, ahead_low, ahead_high],
        tiled=range(6),
    )[0]

    row_losses = lax.dynamic_slice_in_dim(losses[0], at, rows, 0)
    return row_losses, grad_queries, grad_passages


def solution(mesh):
    torus = Mesh(mesh.devices.reshape(mesh.shape[Y], 8, 4, 2), ROW_COL)
    in_specs = (P(ROW_COL, None), P(COL_ROW, None), P(Y), P(Y, None), P(Y))
    out_specs = (P(ROW_COL), P(ROW_COL, None), P(COL_ROW, None))
    return jax.shard_map(
        on_device, mesh=torus, in_specs=in_specs, out_specs=out_specs, check_vma=False
    )
```

```python
import functools

import jax
import jax.numpy as jnp
from jax import lax
from jax.experimental import pallas as pl
from jax.experimental.pallas import tpu as pltpu
from jax.sharding import Mesh
from jax.sharding import PartitionSpec as P

Y, Z, X, CORE = "row", "col_0", "col_1", "col_2"
COL = (Z, X, CORE)
ROW_COL = (Y, Z, X, CORE)
COL_ROW = (Z, X, CORE, Y)

inv_temp = 50.0
sharpness = 4.0
LOWEST = -3.0e38
F32, BF16 = jnp.float32, jnp.bfloat16
TILE = 1024


def shifted(value, axis, step):
    n = lax.axis_size(axis)
    return lax.ppermute(value, axis, [(i, (i + step) % n) for i in range(n)])


def copies(value, axis):
    n = lax.axis_size(axis)
    return lax.all_to_all(jnp.broadcast_to(value, (n, *value.shape)), axis, 0, 0, tiled=True)


def shape(dims, dtype):
    return jax.ShapeDtypeStruct(dims, dtype)


def call(body, outs, args, flops=0, scalars=0, tiled=(), scratch=(), outside=(), tile=TILE):
    size = sum(a.size * a.dtype.itemsize for a in (*args, *outs))
    specs = []
    for k, a in enumerate((*args, *outs)):
        if k < scalars:
            specs.append(pl.BlockSpec(memory_space=pltpu.SMEM))
        elif k in tiled:
            specs.append(pl.BlockSpec((*a.shape[:-1], tile), lambda i, n=len(a.shape): (0,) * (n - 1) + (i,)))
        else:
            specs.append(pl.BlockSpec(a.shape, lambda i, n=len(a.shape): (0,) * n))
    kinds = [pltpu.HBM if k in outside else None for k in range(len(specs))]
    args = [
        a if kind is None else pltpu.with_memory_space_constraint(a, kind)
        for a, kind in zip(args, kinds)
    ]
    outs = [
        o if kind is None else pltpu.HBM(o.shape, o.dtype)
        for o, kind in zip(outs, kinds[len(args) :])
    ]
    steps = (*args, *outs)[tiled[0]].shape[-1] // tile if tiled else 1
    return pl.pallas_call(
        body,
        grid=(steps,),
        out_shape=outs,
        in_specs=specs[: len(args)],
        out_specs=specs[len(args) :],
        scratch_shapes=scratch,
        cost_estimate=pl.CostEstimate(flops=flops, bytes_accessed=size, transcendentals=0),
        compiler_params=pltpu.CompilerParams(vmem_limit_bytes=(24 if flops else 8) << 20),
    )(*args)


def swapped(core, row):
    half = row.shape[1] // 2
    return jnp.where(core == 0, row, jnp.concatenate([row[:, half:], row[:, :half]], axis=1))


def on_step(k):
    return pl.when(pl.program_id(0) == k)


def marks(place, ids, k, lines):
    column = place[1 + k] + lax.broadcasted_iota(jnp.int32, (128, ids.shape[1]), 0)
    found = [column == ids[slot : slot + 1, :] for slot in range(lines)]
    return found[0], functools.reduce(jnp.logical_or, found)


def products(queries, pool, scores):
    @on_step(0)
    def _():
        scores[...] = jnp.zeros_like(scores)

    rows = jnp.concatenate([p[...] for p in pool], axis=0)
    scores[...] += lax.dot_general(
        rows, queries[...], (((1,), (1,)), ((), ())), preferred_element_type=F32
    )


def own_body(own, *refs):
    products(own, refs[:7], refs[7])


def score_body(place, other, *refs):
    pool, own_scores, ids, scores, table, sums = refs[:7], *refs[7:]
    products(other, pool, sums)

    @pl.when(pl.program_id(0) == pl.num_programs(0) - 1)
    def _():
        tops = [[], []]
        for k in range(4):
            rows = slice(128 * k, 128 * k + 128)
            block = jnp.concatenate([own_scores[rows, :], sums[rows, :]], axis=1) * inv_temp
            scores[rows, :] = block
            for top, mark in zip(tops, marks(place, ids, k, 8)):
                top.append(jnp.max(jnp.where(mark, block, LOWEST), axis=0, keepdims=True))
        lines = [swapped(place[0], functools.reduce(jnp.maximum, top)) for top in tops]
        table[...] = jnp.broadcast_to(jnp.concatenate(lines, axis=0)[None], table.shape)


def soft_body(place, table, margin_ref, ids, scores, weights, totals, stats):
    merged = swapped(place[0], jnp.max(table[...], axis=0))
    picked, kept = merged[0:1], merged[1:2]
    margin = margin_ref[0:1, :]
    ceiling = jnp.maximum(kept, picked + margin)
    sums = []
    for k in range(4):
        rows = slice(128 * k, 128 * k + 128)
        block = scores[rows, :]
        over = sharpness * (block - picked - margin)
        penalty = jnp.maximum(over, 0.0) + jnp.log(1.0 + jnp.exp(-jnp.abs(over)))
        logits = jnp.where(marks(place, ids, k, 8)[1], block, block - penalty)
        weight = jnp.exp(logits - ceiling)
        weights[rows, :] = weight
        sums.append(jnp.sum(weight, axis=0, keepdims=True))
    total = swapped(place[0], functools.reduce(jnp.add, sums))
    totals[...] = jnp.broadcast_to(total[None], totals.shape)
    stats[...] = jnp.broadcast_to(ceiling - picked, stats.shape)


def grad_body(place, table, stats, ids, weights, own, other, *refs):
    pool, outs, (grads, turned) = refs[:7], refs[7:17], refs[17:]
    losses, low, high, back_low, back_high, ahead_low, ahead_high, here, mine, theirs = outs

    @on_step(0)
    def _():
        total = swapped(place[0], jnp.sum(table[...], axis=0))
        losses[...] = stats[...] + jnp.log(total)
        for k in range(4):
            rows = slice(128 * k, 128 * k + 128)
            positive = jnp.where(marks(place, ids, k, 1)[0], 1.0, 0.0)
            grads[rows, :] = ((weights[rows, :] / total - positive) * inv_temp).astype(BF16)
        turned[...] = grads[...].T

    columns = jnp.concatenate([own[...], other[...]], axis=0)
    out = jnp.dot(grads[...], columns, preferred_element_type=F32)
    here[...] = out[0:128]
    halves = (back_low, back_high, ahead_low, ahead_high, low, high)
    for k, half in enumerate(halves):
        half[...] = out[128 + 64 * k : 192 + 64 * k].astype(half.dtype)
    rows = jnp.concatenate([p[...] for p in pool], axis=0)
    out = jnp.dot(turned[...], rows, preferred_element_type=F32)
    mine[...] = out[:128]
    theirs[...] = out[128:]


def gathered_body(place, parts, exact, total):
    one = lax.broadcasted_iota(jnp.int32, parts.shape, 0) != place[0]
    total[...] = exact[...] + jnp.sum(jnp.where(one, parts[...].astype(F32), 0.0), axis=0)


def total_body(here, back_low, back_high, ahead_low, ahead_high, total):
    half = back_low.shape[0]
    for rows, parts in (
        (slice(0, half), (back_low, ahead_low)),
        (slice(half, 2 * half), (back_high, ahead_high)),
    ):
        total[rows, :] = here[rows, :] + parts[0][...].astype(F32) + parts[1][...].astype(F32)


def on_device(queries, passages, positives, hard_negatives, thresholds):
    rows, width = queries.shape
    count = passages.shape[0]
    depth, breadth, ring = lax.axis_size(Z), lax.axis_size(X), lax.axis_size(Y)
    core, far, across, along = (lax.axis_index(a) for a in (CORE, Z, X, Y))
    half = count // 2
    plane = depth * breadth * rows
    total, pool, members = 2 * plane, ring * count, 2 * depth * breadth

    low, high = passages[:half], passages[half:]
    back_low, ahead_high = shifted(low, Y, 1), shifted(high, Y, -1)
    back_high, ahead_low = shifted(high, Y, 1), shifted(low, Y, -1)
    line = copies(queries, Z)
    line, back_low, ahead_high = lax.optimization_barrier((line, back_low, ahead_high))
    far_low, far_high = shifted(back_low, Y, 1), shifted(ahead_high, Y, -1)
    own = copies(line.reshape(depth * rows, width), X)

    def ordered(table):
        table = table.reshape(-1, depth, breadth, 2, rows)
        table = jnp.transpose(table, (0, 3, 2, 1, 4)).reshape(-1, 2, plane)
        return jnp.where(core == 0, table, jnp.flip(table, 1)).reshape(-1, total)

    ids = ordered(jnp.concatenate([positives[None, :], hard_negatives.T], axis=0))
    margin = ordered(jnp.broadcast_to(thresholds, (8, total)))
    steps = jnp.array([0, 1, 3, 2], jnp.int32)
    base = (((far * breadth + across) * 2 + core) * ring + (along - steps) % ring) * count
    place = jnp.concatenate([core.reshape(1), base]).astype(jnp.int32)
    own, far_low, far_high, back_high, ahead_low, ids, margin, place = lax.optimization_barrier(
        (own, far_low, far_high, back_high, ahead_low, ids, margin, place)
    )
    own = own.reshape(plane, width)
    other = shifted(own, CORE, 1)
    blocks = [passages, back_low, back_high, ahead_low, ahead_high, far_low, far_high]

    own_scores = call(
        own_body,
        [shape((pool, plane), F32)],
        [own, *blocks],
        flops=2 * plane * pool * width,
        tiled=range(8),
    )[0]
    scores, table = call(
        score_body,
        [shape((pool, total), F32), shape((members, 2, total), F32)],
        [place, other, *blocks, own_scores, ids],
        flops=2 * plane * pool * width,
        scalars=1,
        tiled=range(1, 9),
        scratch=[pltpu.VMEM((pool, plane), F32)],
    )
    table = lax.all_to_all(table, COL, 0, 0, tiled=True)
    weights, table, stats = call(
        soft_body,
        [shape((pool, total), F32), shape((members, 1, total), F32), shape((8, total), F32)],
        [place, table, margin, ids, scores],
        scalars=1,
    )
    table = lax.all_to_all(table, COL, 0, 0, tiled=True)
    sums = [shape((half, width), BF16)] * 6 + [shape((count, width), F32)]
    losses, low, high, back_low, back_high, ahead_low, ahead_high, here, mine, theirs = call(
        grad_body,
        [shape((8, total), F32)] + sums + [shape((plane, width), F32)] * 2,
        [place, table, stats, ids, weights, own, other, *blocks],
        flops=4 * total * pool * width,
        scalars=1,
        tiled=(*range(5, 14), *range(15, 24)),
        scratch=[pltpu.VMEM((pool, total), BF16), pltpu.VMEM((total, pool), BF16)],
        outside=(15, 16, 17, 18, 19, 20, 21, 22, 23),
    )

    low, high = shifted(low, Y, -1), shifted(high, Y, 1)
    back_high, ahead_low = shifted(back_high, Y, -1), shifted(ahead_low, Y, 1)
    theirs = shifted(theirs, CORE, 1)
    back_low = shifted((back_low.astype(F32) + low.astype(F32)).astype(BF16), Y, -1)
    ahead_high = shifted((ahead_high.astype(F32) + high.astype(F32)).astype(BF16), Y, 1)

    place_of = across * depth + far
    at = place_of * rows
    exact = lax.dynamic_slice_in_dim(mine, at, rows, 0) + lax.dynamic_slice_in_dim(theirs, at, rows, 0)
    sent = (mine + theirs).astype(BF16).reshape(breadth * depth, rows, width)
    exact, sent = lax.optimization_barrier((exact, sent))
    parts = lax.all_to_all(sent, (X, Z), 0, 0, tiled=True)
    grad_queries = call(
        gathered_body,
        [shape((rows, width), F32)],
        [place_of.reshape(1).astype(jnp.int32), parts, exact],
        scalars=1,
        tiled=(1, 2, 3),
    )[0]

    grad_passages = call(
        total_body,
        [shape((count, width), F32)],
        [here, back_low, back_high, ahead_low, ahead_high],
        tiled=range(6),
        tile=2048,
    )[0]

    row_losses = lax.dynamic_slice_in_dim(losses[0], at, rows, 0)
    return row_losses, grad_queries, grad_passages


def solution(mesh):
    torus = Mesh(mesh.devices.reshape(mesh.shape[Y], 8, 4, 2), ROW_COL)
    in_specs = (P(ROW_COL, None), P(COL_ROW, None), P(Y), P(Y, None), P(Y))
    out_specs = (P(ROW_COL), P(ROW_COL, None), P(COL_ROW, None))
    return jax.shard_map(
        on_device, mesh=torus, in_specs=in_specs, out_specs=out_specs, check_vma=False
    )
```

```python
import functools

import jax
import jax.numpy as jnp
from jax import lax
from jax.experimental import pallas as pl
from jax.experimental.pallas import tpu as pltpu
from jax.sharding import Mesh
from jax.sharding import PartitionSpec as P

Y, Z, X, CORE = "row", "col_0", "col_1", "col_2"
COL = (Z, X, CORE)
ROW_COL = (Y, Z, X, CORE)
COL_ROW = (Z, X, CORE, Y)

inv_temp = 50.0
sharpness = 4.0
LOWEST = -3.0e38
F32, BF16 = jnp.float32, jnp.bfloat16
TILE = 1024


def shifted(value, axis, step):
    n = lax.axis_size(axis)
    return lax.ppermute(value, axis, [(i, (i + step) % n) for i in range(n)])


def copies(value, axis):
    n = lax.axis_size(axis)
    return lax.all_to_all(jnp.broadcast_to(value, (n, *value.shape)), axis, 0, 0, tiled=True)


def shape(dims, dtype):
    return jax.ShapeDtypeStruct(dims, dtype)


def call(body, outs, args, flops=0, scalars=0, tiled=(), scratch=(), outside=(), tile=TILE):
    size = sum(a.size * a.dtype.itemsize for a in (*args, *outs))
    specs = []
    for k, a in enumerate((*args, *outs)):
        if k < scalars:
            specs.append(pl.BlockSpec(memory_space=pltpu.SMEM))
        elif k in tiled:
            specs.append(pl.BlockSpec((*a.shape[:-1], tile), lambda i, n=len(a.shape): (0,) * (n - 1) + (i,)))
        else:
            specs.append(pl.BlockSpec(a.shape, lambda i, n=len(a.shape): (0,) * n))
    kinds = [pltpu.HBM if k in outside else None for k in range(len(specs))]
    args = [
        a if kind is None else pltpu.with_memory_space_constraint(a, kind)
        for a, kind in zip(args, kinds)
    ]
    outs = [
        o if kind is None else pltpu.HBM(o.shape, o.dtype)
        for o, kind in zip(outs, kinds[len(args) :])
    ]
    steps = (*args, *outs)[tiled[0]].shape[-1] // tile if tiled else 1
    return pl.pallas_call(
        body,
        grid=(steps,),
        out_shape=outs,
        in_specs=specs[: len(args)],
        out_specs=specs[len(args) :],
        scratch_shapes=scratch,
        cost_estimate=pl.CostEstimate(flops=flops, bytes_accessed=size, transcendentals=0),
        compiler_params=pltpu.CompilerParams(vmem_limit_bytes=(24 if flops else 8) << 20),
    )(*args)


def swapped(core, row):
    half = row.shape[1] // 2
    return jnp.where(core == 0, row, jnp.concatenate([row[:, half:], row[:, :half]], axis=1))


def on_step(k):
    return pl.when(pl.program_id(0) == k)


def marks(place, ids, k, lines):
    column = place[1 + k] + lax.broadcasted_iota(jnp.int32, (128, ids.shape[1]), 0)
    found = [column == ids[slot : slot + 1, :] for slot in range(lines)]
    return found[0], functools.reduce(jnp.logical_or, found)


def score_body(place, own, other, *refs):
    pool, ids, scores, table = refs[:7], *refs[7:]

    @on_step(0)
    def _():
        scores[...] = jnp.zeros_like(scores)

    rows = jnp.concatenate([p[...] for p in pool], axis=0)
    columns = jnp.concatenate([own[...], other[...]], axis=0)
    scores[...] += lax.dot_general(
        rows, columns, (((1,), (1,)), ((), ())), preferred_element_type=F32
    )

    @pl.when(pl.program_id(0) == pl.num_programs(0) - 1)
    def _():
        tops = [[], []]
        for k in range(4):
            rows = slice(128 * k, 128 * k + 128)
            block = scores[rows, :] * inv_temp
            scores[rows, :] = block
            for top, mark in zip(tops, marks(place, ids, k, 8)):
                top.append(jnp.max(jnp.where(mark, block, LOWEST), axis=0, keepdims=True))
        lines = [swapped(place[0], functools.reduce(jnp.maximum, top)) for top in tops]
        table[...] = jnp.broadcast_to(jnp.concatenate(lines, axis=0)[None], table.shape)


def soft_body(place, table, margin_ref, ids, scores, weights, totals, stats):
    merged = swapped(place[0], jnp.max(table[...], axis=0))
    picked, kept = merged[0:1], merged[1:2]
    margin = margin_ref[0:1, :]
    ceiling = jnp.maximum(kept, picked + margin)
    sums = []
    for k in range(4):
        rows = slice(128 * k, 128 * k + 128)
        block = scores[rows, :]
        over = sharpness * (block - picked - margin)
        penalty = jnp.maximum(over, 0.0) + jnp.log(1.0 + jnp.exp(-jnp.abs(over)))
        logits = jnp.where(marks(place, ids, k, 8)[1], block, block - penalty)
        weight = jnp.exp(logits - ceiling)
        weights[rows, :] = weight
        sums.append(jnp.sum(weight, axis=0, keepdims=True))
    total = swapped(place[0], functools.reduce(jnp.add, sums))
    totals[...] = jnp.broadcast_to(total[None], totals.shape)
    stats[...] = jnp.broadcast_to(ceiling - picked, stats.shape)


def grad_body(place, table, stats, ids, weights, own, other, *refs):
    pool, outs, (grads, turned) = refs[:7], refs[7:17], refs[17:]
    losses, low, high, back_low, back_high, ahead_low, ahead_high, here, mine, theirs = outs

    @on_step(0)
    def _():
        total = swapped(place[0], jnp.sum(table[...], axis=0))
        losses[...] = stats[...] + jnp.log(total)
        for k in range(4):
            rows = slice(128 * k, 128 * k + 128)
            positive = jnp.where(marks(place, ids, k, 1)[0], 1.0, 0.0)
            grads[rows, :] = ((weights[rows, :] / total - positive) * inv_temp).astype(BF16)
        turned[...] = grads[...].T

    columns = jnp.concatenate([own[...], other[...]], axis=0)
    out = jnp.dot(grads[...], columns, preferred_element_type=F32)
    here[...] = out[0:128]
    halves = (back_low, back_high, ahead_low, ahead_high, low, high)
    for k, half in enumerate(halves):
        half[...] = out[128 + 64 * k : 192 + 64 * k].astype(half.dtype)
    rows = jnp.concatenate([p[...] for p in pool], axis=0)
    out = jnp.dot(turned[...], rows, preferred_element_type=F32)
    mine[...] = out[:128]
    theirs[...] = out[128:]


def gathered_body(place, parts, exact, total):
    one = lax.broadcasted_iota(jnp.int32, parts.shape, 0) != place[0]
    total[...] = exact[...] + jnp.sum(jnp.where(one, parts[...].astype(F32), 0.0), axis=0)


def total_body(here, back_low, back_high, ahead_low, ahead_high, total):
    half = back_low.shape[0]
    for rows, parts in (
        (slice(0, half), (back_low, ahead_low)),
        (slice(half, 2 * half), (back_high, ahead_high)),
    ):
        total[rows, :] = here[rows, :] + parts[0][...].astype(F32) + parts[1][...].astype(F32)


def on_device(queries, passages, positives, hard_negatives, thresholds):
    rows, width = queries.shape
    count = passages.shape[0]
    depth, breadth, ring = lax.axis_size(Z), lax.axis_size(X), lax.axis_size(Y)
    core, far, across, along = (lax.axis_index(a) for a in (CORE, Z, X, Y))
    half = count // 2
    plane = depth * breadth * rows
    total, pool, members = 2 * plane, ring * count, 2 * depth * breadth

    low, high = passages[:half], passages[half:]
    back_low, ahead_high = shifted(low, Y, 1), shifted(high, Y, -1)
    back_high, ahead_low = shifted(high, Y, 1), shifted(low, Y, -1)
    line = copies(queries, Z)
    line, back_low, ahead_high = lax.optimization_barrier((line, back_low, ahead_high))
    far_low, far_high = shifted(back_low, Y, 1), shifted(ahead_high, Y, -1)
    own = copies(line.reshape(depth * rows, width), X)

    def ordered(table):
        table = table.reshape(-1, depth, breadth, 2, rows)
        table = jnp.transpose(table, (0, 3, 2, 1, 4)).reshape(-1, 2, plane)
        return jnp.where(core == 0, table, jnp.flip(table, 1)).reshape(-1, total)

    ids = ordered(jnp.concatenate([positives[None, :], hard_negatives.T], axis=0))
    margin = ordered(jnp.broadcast_to(thresholds, (8, total)))
    steps = jnp.array([0, 1, 3, 2], jnp.int32)
    base = (((far * breadth + across) * 2 + core) * ring + (along - steps) % ring) * count
    place = jnp.concatenate([core.reshape(1), base]).astype(jnp.int32)
    own, far_low, far_high, back_high, ahead_low, ids, margin, place = lax.optimization_barrier(
        (own, far_low, far_high, back_high, ahead_low, ids, margin, place)
    )
    own = own.reshape(plane, width)
    other = shifted(own, CORE, 1)
    blocks = [passages, back_low, back_high, ahead_low, ahead_high, far_low, far_high]

    scores, table = call(
        score_body,
        [shape((pool, total), F32), shape((members, 2, total), F32)],
        [place, own, other, *blocks, ids],
        flops=2 * total * pool * width,
        scalars=1,
        tiled=range(1, 10),
        tile=2048,
    )
    table = lax.all_to_all(table, COL, 0, 0, tiled=True)
    weights, table, stats = call(
        soft_body,
        [shape((pool, total), F32), shape((members, 1, total), F32), shape((8, total), F32)],
        [place, table, margin, ids, scores],
        scalars=1,
    )
    table = lax.all_to_all(table, COL, 0, 0, tiled=True)
    sums = [shape((half, width), BF16)] * 6 + [shape((count, width), F32)]
    losses, low, high, back_low, back_high, ahead_low, ahead_high, here, mine, theirs = call(
        grad_body,
        [shape((8, total), F32)] + sums + [shape((plane, width), F32)] * 2,
        [place, table, stats, ids, weights, own, other, *blocks],
        flops=4 * total * pool * width,
        scalars=1,
        tiled=(*range(5, 14), *range(15, 24)),
        tile=2048,
        scratch=[pltpu.VMEM((pool, total), BF16), pltpu.VMEM((total, pool), BF16)],
        outside=(15, 16, 17, 18, 19, 20, 21, 22, 23),
    )

    low, high = shifted(low, Y, -1), shifted(high, Y, 1)
    back_high, ahead_low = shifted(back_high, Y, -1), shifted(ahead_low, Y, 1)
    theirs = shifted(theirs, CORE, 1)
    back_low = shifted((back_low.astype(F32) + low.astype(F32)).astype(BF16), Y, -1)
    ahead_high = shifted((ahead_high.astype(F32) + high.astype(F32)).astype(BF16), Y, 1)

    place_of = across * depth + far
    at = place_of * rows
    exact = lax.dynamic_slice_in_dim(mine, at, rows, 0) + lax.dynamic_slice_in_dim(theirs, at, rows, 0)
    sent = (mine + theirs).astype(BF16).reshape(breadth * depth, rows, width)
    exact, sent = lax.optimization_barrier((exact, sent))
    parts = lax.all_to_all(sent, (X, Z), 0, 0, tiled=True)
    grad_queries = call(
        gathered_body,
        [shape((rows, width), F32)],
        [place_of.reshape(1).astype(jnp.int32), parts, exact],
        scalars=1,
        tiled=(1, 2, 3),
    )[0]

    grad_passages = call(
        total_body,
        [shape((count, width), F32)],
        [here, back_low, back_high, ahead_low, ahead_high],
        tiled=range(6),
        tile=2048,
    )[0]

    row_losses = lax.dynamic_slice_in_dim(losses[0], at, rows, 0)
    return row_losses, grad_queries, grad_passages


def solution(mesh):
    torus = Mesh(mesh.devices.reshape(mesh.shape[Y], 8, 4, 2), ROW_COL)
    in_specs = (P(ROW_COL, None), P(COL_ROW, None), P(Y), P(Y, None), P(Y))
    out_specs = (P(ROW_COL), P(ROW_COL, None), P(COL_ROW, None))
    return jax.shard_map(
        on_device, mesh=torus, in_specs=in_specs, out_specs=out_specs, check_vma=False
    )
```

```python
import functools

import jax
import jax.numpy as jnp
from jax import lax
from jax.experimental import pallas as pl
from jax.experimental.pallas import tpu as pltpu
from jax.sharding import Mesh
from jax.sharding import PartitionSpec as P

Y, Z, X, CORE = "row", "col_0", "col_1", "col_2"
COL = (Z, X, CORE)
ROW_COL = (Y, Z, X, CORE)
COL_ROW = (Z, X, CORE, Y)

inv_temp = 50.0
sharpness = 4.0
LOWEST = -3.0e38
F32, BF16 = jnp.float32, jnp.bfloat16
TILE = 1024


def shifted(value, axis, step):
    n = lax.axis_size(axis)
    return lax.ppermute(value, axis, [(i, (i + step) % n) for i in range(n)])


def copies(value, axis):
    n = lax.axis_size(axis)
    return lax.all_to_all(jnp.broadcast_to(value, (n, *value.shape)), axis, 0, 0, tiled=True)


def shape(dims, dtype):
    return jax.ShapeDtypeStruct(dims, dtype)


def call(body, outs, args, flops=0, scalars=0, tiled=(), scratch=(), outside=(), tile=TILE):
    size = sum(a.size * a.dtype.itemsize for a in (*args, *outs))
    specs = []
    for k, a in enumerate((*args, *outs)):
        if k < scalars:
            specs.append(pl.BlockSpec(memory_space=pltpu.SMEM))
        elif k in tiled:
            specs.append(pl.BlockSpec((*a.shape[:-1], tile), lambda i, n=len(a.shape): (0,) * (n - 1) + (i,)))
        else:
            specs.append(pl.BlockSpec(a.shape, lambda i, n=len(a.shape): (0,) * n))
    kinds = [pltpu.HBM if k in outside else None for k in range(len(specs))]
    args = [
        a if kind is None else pltpu.with_memory_space_constraint(a, kind)
        for a, kind in zip(args, kinds)
    ]
    outs = [
        o if kind is None else pltpu.HBM(o.shape, o.dtype)
        for o, kind in zip(outs, kinds[len(args) :])
    ]
    steps = (*args, *outs)[tiled[0]].shape[-1] // tile if tiled else 1
    return pl.pallas_call(
        body,
        grid=(steps,),
        out_shape=outs,
        in_specs=specs[: len(args)],
        out_specs=specs[len(args) :],
        scratch_shapes=scratch,
        cost_estimate=pl.CostEstimate(flops=flops, bytes_accessed=size, transcendentals=0),
        compiler_params=pltpu.CompilerParams(vmem_limit_bytes=(24 if flops else 8) << 20),
    )(*args)


def swapped(core, row):
    half = row.shape[1] // 2
    return jnp.where(core == 0, row, jnp.concatenate([row[:, half:], row[:, :half]], axis=1))


def on_step(k):
    return pl.when(pl.program_id(0) == k)


def marks(place, ids, k, lines):
    column = place[1 + k] + lax.broadcasted_iota(jnp.int32, (128, ids.shape[1]), 0)
    found = [column == ids[slot : slot + 1, :] for slot in range(lines)]
    return found[0], functools.reduce(jnp.logical_or, found)


def score_body(place, own, other, *refs):
    pool, ids, scores, table = refs[:7], *refs[7:]

    @on_step(0)
    def _():
        scores[...] = jnp.zeros_like(scores)

    rows = jnp.concatenate([p[...] for p in pool], axis=0)
    columns = jnp.concatenate([own[...], other[...]], axis=0)
    scores[...] += lax.dot_general(
        rows, columns, (((1,), (1,)), ((), ())), preferred_element_type=F32
    )

    @pl.when(pl.program_id(0) == pl.num_programs(0) - 1)
    def _():
        tops = [[], []]
        for k in range(4):
            rows = slice(128 * k, 128 * k + 128)
            block = scores[rows, :] * inv_temp
            scores[rows, :] = block
            for top, mark in zip(tops, marks(place, ids, k, 8)):
                top.append(jnp.max(jnp.where(mark, block, LOWEST), axis=0, keepdims=True))
        lines = [swapped(place[0], functools.reduce(jnp.maximum, top)) for top in tops]
        table[...] = jnp.broadcast_to(jnp.concatenate(lines, axis=0)[None], table.shape)


def soft_body(place, table, margin_ref, ids, scores, weights, totals, stats):
    merged = swapped(place[0], jnp.max(table[...], axis=0))
    picked, kept = merged[0:1], merged[1:2]
    margin = margin_ref[0:1, :]
    ceiling = jnp.maximum(kept, picked + margin)
    sums = []
    for k in range(4):
        rows = slice(128 * k, 128 * k + 128)
        block = scores[rows, :]
        over = sharpness * (block - picked - margin)
        penalty = jnp.maximum(over, 0.0) + jnp.log(1.0 + jnp.exp(-jnp.abs(over)))
        logits = jnp.where(marks(place, ids, k, 8)[1], block, block - penalty)
        weight = jnp.exp(logits - ceiling)
        weights[rows, :] = weight
        sums.append(jnp.sum(weight, axis=0, keepdims=True))
    total = swapped(place[0], functools.reduce(jnp.add, sums))
    totals[...] = jnp.broadcast_to(total[None], totals.shape)
    stats[...] = jnp.broadcast_to(ceiling - picked, stats.shape)


def grad_body(place, table, stats, ids, weights, own, other, *refs):
    pool, outs, (grads, turned) = refs[:7], refs[7:17], refs[17:]
    losses, low, high, back_low, back_high, ahead_low, ahead_high, here, mine, theirs = outs

    @on_step(0)
    def _():
        total = swapped(place[0], jnp.sum(table[...], axis=0))
        losses[...] = stats[...] + jnp.log(total)
        for k in range(4):
            rows = slice(128 * k, 128 * k + 128)
            positive = jnp.where(marks(place, ids, k, 1)[0], 1.0, 0.0)
            grads[rows, :] = ((weights[rows, :] / total - positive) * inv_temp).astype(BF16)
        turned[...] = grads[...].T

    columns = jnp.concatenate([own[...], other[...]], axis=0)
    out = jnp.dot(grads[...], columns, preferred_element_type=F32)
    here[...] = out[0:128]
    halves = (back_low, back_high, ahead_low, ahead_high, low, high)
    for k, half in enumerate(halves):
        half[...] = out[128 + 64 * k : 192 + 64 * k].astype(half.dtype)
    rows = jnp.concatenate([p[...] for p in pool], axis=0)
    out = jnp.dot(turned[...], rows, preferred_element_type=F32)
    mine[...] = out[:128]
    theirs[...] = out[128:]


def gathered_body(place, parts, exact, total):
    one = lax.broadcasted_iota(jnp.int32, parts.shape, 0) != place[0]
    total[...] = exact[...] + jnp.sum(jnp.where(one, parts[...].astype(F32), 0.0), axis=0)


def total_body(here, back_low, back_high, ahead_low, ahead_high, total):
    half = back_low.shape[0]
    for rows, parts in (
        (slice(0, half), (back_low, ahead_low)),
        (slice(half, 2 * half), (back_high, ahead_high)),
    ):
        total[rows, :] = here[rows, :] + parts[0][...].astype(F32) + parts[1][...].astype(F32)


def on_device(queries, passages, positives, hard_negatives, thresholds):
    rows, width = queries.shape
    count = passages.shape[0]
    depth, breadth, ring = lax.axis_size(Z), lax.axis_size(X), lax.axis_size(Y)
    core, far, across, along = (lax.axis_index(a) for a in (CORE, Z, X, Y))
    half = count // 2
    plane = depth * breadth * rows
    total, pool, members = 2 * plane, ring * count, 2 * depth * breadth

    low, high = passages[:half], passages[half:]
    back_low, ahead_high = shifted(low, Y, 1), shifted(high, Y, -1)
    back_high, ahead_low = shifted(high, Y, 1), shifted(low, Y, -1)
    line = copies(queries, Z)
    line, back_low, ahead_high = lax.optimization_barrier((line, back_low, ahead_high))
    far_low, far_high = shifted(back_low, Y, 1), shifted(ahead_high, Y, -1)
    own = copies(line.reshape(depth * rows, width), X)

    def ordered(table):
        table = table.reshape(-1, depth, breadth, 2, rows)
        table = jnp.transpose(table, (0, 3, 2, 1, 4)).reshape(-1, 2, plane)
        return jnp.where(core == 0, table, jnp.flip(table, 1)).reshape(-1, total)

    ids = ordered(jnp.concatenate([positives[None, :], hard_negatives.T], axis=0))
    margin = ordered(jnp.broadcast_to(thresholds, (8, total)))
    steps = jnp.array([0, 1, 3, 2], jnp.int32)
    base = (((far * breadth + across) * 2 + core) * ring + (along - steps) % ring) * count
    place = jnp.concatenate([core.reshape(1), base]).astype(jnp.int32)
    own, far_low, far_high, back_high, ahead_low, ids, margin, place = lax.optimization_barrier(
        (own, far_low, far_high, back_high, ahead_low, ids, margin, place)
    )
    own = own.reshape(plane, width)
    other = shifted(own, CORE, 1)
    blocks = [passages, back_low, back_high, ahead_low, ahead_high, far_low, far_high]

    scores, table = call(
        score_body,
        [shape((pool, total), F32), shape((members, 2, total), F32)],
        [place, own, other, *blocks, ids],
        flops=2 * total * pool * width,
        scalars=1,
        tiled=range(1, 10),
        tile=4096,
    )
    table = lax.all_to_all(table, COL, 0, 0, tiled=True)
    weights, table, stats = call(
        soft_body,
        [shape((pool, total), F32), shape((members, 1, total), F32), shape((8, total), F32)],
        [place, table, margin, ids, scores],
        scalars=1,
    )
    table = lax.all_to_all(table, COL, 0, 0, tiled=True)
    sums = [shape((half, width), BF16)] * 6 + [shape((count, width), F32)]
    losses, low, high, back_low, back_high, ahead_low, ahead_high, here, mine, theirs = call(
        grad_body,
        [shape((8, total), F32)] + sums + [shape((plane, width), F32)] * 2,
        [place, table, stats, ids, weights, own, other, *blocks],
        flops=4 * total * pool * width,
        scalars=1,
        tiled=(*range(5, 14), *range(15, 24)),
        tile=2048,
        scratch=[pltpu.VMEM((pool, total), BF16), pltpu.VMEM((total, pool), BF16)],
        outside=(15, 16, 17, 18, 19, 20, 21, 22, 23),
    )

    low, high = shifted(low, Y, -1), shifted(high, Y, 1)
    back_high, ahead_low = shifted(back_high, Y, -1), shifted(ahead_low, Y, 1)
    theirs = shifted(theirs, CORE, 1)
    back_low = shifted((back_low.astype(F32) + low.astype(F32)).astype(BF16), Y, -1)
    ahead_high = shifted((ahead_high.astype(F32) + high.astype(F32)).astype(BF16), Y, 1)

    place_of = across * depth + far
    at = place_of * rows
    exact = lax.dynamic_slice_in_dim(mine, at, rows, 0) + lax.dynamic_slice_in_dim(theirs, at, rows, 0)
    sent = (mine + theirs).astype(BF16).reshape(breadth * depth, rows, width)
    exact, sent = lax.optimization_barrier((exact, sent))
    parts = lax.all_to_all(sent, (X, Z), 0, 0, tiled=True)
    grad_queries = call(
        gathered_body,
        [shape((rows, width), F32)],
        [place_of.reshape(1).astype(jnp.int32), parts, exact],
        scalars=1,
        tiled=(1, 2, 3),
        tile=2048,
    )[0]

    grad_passages = call(
        total_body,
        [shape((count, width), F32)],
        [here, back_low, back_high, ahead_low, ahead_high],
        tiled=range(6),
        tile=4096,
    )[0]

    row_losses = lax.dynamic_slice_in_dim(losses[0], at, rows, 0)
    return row_losses, grad_queries, grad_passages


def solution(mesh):
    torus = Mesh(mesh.devices.reshape(mesh.shape[Y], 8, 4, 2), ROW_COL)
    in_specs = (P(ROW_COL, None), P(COL_ROW, None), P(Y), P(Y, None), P(Y))
    out_specs = (P(ROW_COL), P(ROW_COL, None), P(COL_ROW, None))
    return jax.shard_map(
        on_device, mesh=torus, in_specs=in_specs, out_specs=out_specs, check_vma=False
    )
```

```python
import functools

import jax
import jax.numpy as jnp
from jax import lax
from jax.experimental import pallas as pl
from jax.experimental.pallas import tpu as pltpu
from jax.sharding import Mesh
from jax.sharding import PartitionSpec as P

Y, Z, X, CORE = "row", "col_0", "col_1", "col_2"
COL = (Z, X, CORE)
ROW_COL = (Y, Z, X, CORE)
COL_ROW = (Z, X, CORE, Y)

inv_temp = 50.0
sharpness = 4.0
LOWEST = -3.0e38
F32, BF16 = jnp.float32, jnp.bfloat16
TILE = 1024


def shifted(value, axis, step):
    n = lax.axis_size(axis)
    return lax.ppermute(value, axis, [(i, (i + step) % n) for i in range(n)])


def copies(value, axis):
    n = lax.axis_size(axis)
    return lax.all_to_all(jnp.broadcast_to(value, (n, *value.shape)), axis, 0, 0, tiled=True)


def shape(dims, dtype):
    return jax.ShapeDtypeStruct(dims, dtype)


def call(body, outs, args, flops=0, scalars=0, tiled=(), scratch=(), outside=(), tile=TILE):
    size = sum(a.size * a.dtype.itemsize for a in (*args, *outs))
    specs = []
    for k, a in enumerate((*args, *outs)):
        if k < scalars:
            specs.append(pl.BlockSpec(memory_space=pltpu.SMEM))
        elif k in tiled:
            specs.append(pl.BlockSpec((*a.shape[:-1], tile), lambda i, n=len(a.shape): (0,) * (n - 1) + (i,)))
        else:
            specs.append(pl.BlockSpec(a.shape, lambda i, n=len(a.shape): (0,) * n))
    kinds = [pltpu.HBM if k in outside else None for k in range(len(specs))]
    args = [
        a if kind is None else pltpu.with_memory_space_constraint(a, kind)
        for a, kind in zip(args, kinds)
    ]
    outs = [
        o if kind is None else pltpu.HBM(o.shape, o.dtype)
        for o, kind in zip(outs, kinds[len(args) :])
    ]
    steps = (*args, *outs)[tiled[0]].shape[-1] // tile if tiled else 1
    return pl.pallas_call(
        body,
        grid=(steps,),
        out_shape=outs,
        in_specs=specs[: len(args)],
        out_specs=specs[len(args) :],
        scratch_shapes=scratch,
        cost_estimate=pl.CostEstimate(flops=flops, bytes_accessed=size, transcendentals=0),
        compiler_params=pltpu.CompilerParams(vmem_limit_bytes=(24 if flops else 8) << 20),
    )(*args)


def swapped(core, row):
    half = row.shape[1] // 2
    return jnp.where(core == 0, row, jnp.concatenate([row[:, half:], row[:, :half]], axis=1))


def on_step(k):
    return pl.when(pl.program_id(0) == k)


def marks(place, ids, k, lines):
    column = place[1 + k] + lax.broadcasted_iota(jnp.int32, (128, ids.shape[1]), 0)
    found = [column == ids[slot : slot + 1, :] for slot in range(lines)]
    return found[0], functools.reduce(jnp.logical_or, found)


def score_body(place, own, other, *refs):
    pool, ids, scores, table = refs[:7], *refs[7:]

    @on_step(0)
    def _():
        scores[...] = jnp.zeros_like(scores)

    rows = jnp.concatenate([p[...] for p in pool], axis=0)
    columns = jnp.concatenate([own[...], other[...]], axis=0)
    scores[...] += lax.dot_general(
        rows, columns, (((1,), (1,)), ((), ())), preferred_element_type=F32
    )

    @pl.when(pl.program_id(0) == pl.num_programs(0) - 1)
    def _():
        tops = [[], []]
        for k in range(4):
            rows = slice(128 * k, 128 * k + 128)
            block = scores[rows, :] * inv_temp
            scores[rows, :] = block
            for top, mark in zip(tops, marks(place, ids, k, 8)):
                top.append(jnp.max(jnp.where(mark, block, LOWEST), axis=0, keepdims=True))
        lines = [swapped(place[0], functools.reduce(jnp.maximum, top)) for top in tops]
        table[...] = jnp.broadcast_to(jnp.concatenate(lines, axis=0)[None], table.shape)


def soft_body(place, table, margin_ref, ids, scores, weights, totals, stats):
    merged = swapped(place[0], jnp.max(table[...], axis=0))
    picked, kept = merged[0:1], merged[1:2]
    margin = margin_ref[0:1, :]
    ceiling = jnp.maximum(kept, picked + margin)
    sums = []
    for k in range(4):
        rows = slice(128 * k, 128 * k + 128)
        block = scores[rows, :]
        over = sharpness * (block - picked - margin)
        penalty = jnp.maximum(over, 0.0) + jnp.log(1.0 + jnp.exp(-jnp.abs(over)))
        logits = jnp.where(marks(place, ids, k, 8)[1], block, block - penalty)
        weight = jnp.exp(logits - ceiling)
        weights[rows, :] = weight
        sums.append(jnp.sum(weight, axis=0, keepdims=True))
    total = swapped(place[0], functools.reduce(jnp.add, sums))
    totals[...] = jnp.broadcast_to(total[None], totals.shape)
    stats[...] = jnp.broadcast_to(ceiling - picked, stats.shape)


def grad_body(place, table, stats, ids, weights, own, other, *refs):
    pool, outs, (grads, turned) = refs[:7], refs[7:17], refs[17:]
    losses, low, high, back_low, back_high, ahead_low, ahead_high, here, mine, theirs = outs

    @on_step(0)
    def _():
        total = swapped(place[0], jnp.sum(table[...], axis=0))
        losses[...] = stats[...] + jnp.log(total)
        for k in range(4):
            rows = slice(128 * k, 128 * k + 128)
            positive = jnp.where(marks(place, ids, k, 1)[0], 1.0, 0.0)
            grads[rows, :] = ((weights[rows, :] / total - positive) * inv_temp).astype(BF16)
        turned[...] = grads[...].T

    columns = jnp.concatenate([own[...], other[...]], axis=0)
    out = jnp.dot(grads[...], columns, preferred_element_type=F32)
    here[...] = out[0:128]
    halves = (back_low, back_high, ahead_low, ahead_high, low, high)
    for k, half in enumerate(halves):
        half[...] = out[128 + 64 * k : 192 + 64 * k].astype(half.dtype)
    rows = jnp.concatenate([p[...] for p in pool], axis=0)
    out = jnp.dot(turned[...], rows, preferred_element_type=F32)
    mine[...] = out[:128]
    theirs[...] = out[128:]


def gathered_body(place, parts, exact, total):
    one = lax.broadcasted_iota(jnp.int32, parts.shape, 0) != place[0]
    total[...] = exact[...] + jnp.sum(jnp.where(one, parts[...].astype(F32), 0.0), axis=0)


def total_body(here, back_low, back_high, ahead_low, ahead_high, total):
    half = back_low.shape[0]
    for rows, parts in (
        (slice(0, half), (back_low, ahead_low)),
        (slice(half, 2 * half), (back_high, ahead_high)),
    ):
        total[rows, :] = here[rows, :] + parts[0][...].astype(F32) + parts[1][...].astype(F32)


def on_device(queries, passages, positives, hard_negatives, thresholds):
    rows, width = queries.shape
    count = passages.shape[0]
    depth, breadth, ring = lax.axis_size(Z), lax.axis_size(X), lax.axis_size(Y)
    core, far, across, along = (lax.axis_index(a) for a in (CORE, Z, X, Y))
    half = count // 2
    plane = depth * breadth * rows
    total, pool, members = 2 * plane, ring * count, 2 * depth * breadth

    low, high = passages[:half], passages[half:]
    back_low, ahead_high = shifted(low, Y, 1), shifted(high, Y, -1)
    back_high, ahead_low = shifted(high, Y, 1), shifted(low, Y, -1)
    line = copies(queries, Z)
    line, back_low, ahead_high = lax.optimization_barrier((line, back_low, ahead_high))
    far_low, far_high = shifted(back_low, Y, 1), shifted(ahead_high, Y, -1)
    own = copies(line.reshape(depth * rows, width), X)

    def ordered(table):
        table = table.reshape(-1, depth, breadth, 2, rows)
        table = jnp.transpose(table, (0, 3, 2, 1, 4)).reshape(-1, 2, plane)
        return jnp.where(core == 0, table, jnp.flip(table, 1)).reshape(-1, total)

    ids = ordered(jnp.concatenate([positives[None, :], hard_negatives.T], axis=0))
    margin = ordered(jnp.broadcast_to(thresholds, (8, total)))
    steps = jnp.array([0, 1, 3, 2], jnp.int32)
    base = (((far * breadth + across) * 2 + core) * ring + (along - steps) % ring) * count
    place = jnp.concatenate([core.reshape(1), base]).astype(jnp.int32)
    own, far_low, far_high, back_high, ahead_low, ids, margin, place = lax.optimization_barrier(
        (own, far_low, far_high, back_high, ahead_low, ids, margin, place)
    )
    own = own.reshape(plane, width)
    other = shifted(own, CORE, 1)
    blocks = [passages, back_low, back_high, ahead_low, ahead_high, far_low, far_high]

    scores, table = call(
        score_body,
        [shape((pool, total), F32), shape((members, 2, total), F32)],
        [place, own, other, *blocks, ids],
        flops=2 * total * pool * width,
        scalars=1,
        tiled=range(1, 10),
        tile=4096,
    )
    table = lax.all_to_all(table, COL, 0, 0, tiled=True)
    weights, table, stats = call(
        soft_body,
        [shape((pool, total), F32), shape((members, 1, total), F32), shape((8, total), F32)],
        [place, table, margin, ids, scores],
        scalars=1,
    )
    table = lax.all_to_all(table, COL, 0, 0, tiled=True)
    sums = [shape((half, width), BF16)] * 6 + [shape((count, width), F32)]
    losses, low, high, back_low, back_high, ahead_low, ahead_high, here, mine, theirs = call(
        grad_body,
        [shape((8, total), F32)] + sums + [shape((plane, width), F32)] * 2,
        [place, table, stats, ids, weights, own, other, *blocks],
        flops=4 * total * pool * width,
        scalars=1,
        tiled=(*range(5, 14), *range(15, 24)),
        tile=2048,
        scratch=[pltpu.VMEM((pool, total), BF16), pltpu.VMEM((total, pool), BF16)],
        outside=(15, 16, 17, 18, 19, 20, 21, 22, 23),
    )

    low, high = shifted(low, Y, -1), shifted(high, Y, 1)
    back_high, ahead_low = shifted(back_high, Y, -1), shifted(ahead_low, Y, 1)
    theirs = shifted(theirs, CORE, 1)
    back_low = shifted((back_low.astype(F32) + low.astype(F32)).astype(BF16), Y, -1)
    ahead_high = shifted((ahead_high.astype(F32) + high.astype(F32)).astype(BF16), Y, 1)

    place_of = across * depth + far
    at = place_of * rows
    exact = lax.dynamic_slice_in_dim(mine, at, rows, 0) + lax.dynamic_slice_in_dim(theirs, at, rows, 0)
    sent = (mine + theirs).astype(BF16).reshape(breadth * depth, rows, width)
    exact, sent = lax.optimization_barrier((exact, sent))
    parts = lax.all_to_all(sent, (X, Z), 0, 0, tiled=True)
    grad_queries = call(
        gathered_body,
        [shape((rows, width), F32)],
        [place_of.reshape(1).astype(jnp.int32), parts, exact],
        scalars=1,
        tiled=(1, 2, 3),
        tile=4096,
    )[0]

    grad_passages = call(
        total_body,
        [shape((count, width), F32)],
        [here, back_low, back_high, ahead_low, ahead_high],
        tiled=range(6),
        tile=2048,
    )[0]

    row_losses = lax.dynamic_slice_in_dim(losses[0], at, rows, 0)
    return row_losses, grad_queries, grad_passages


def solution(mesh):
    torus = Mesh(mesh.devices.reshape(mesh.shape[Y], 8, 4, 2), ROW_COL)
    in_specs = (P(ROW_COL, None), P(COL_ROW, None), P(Y), P(Y, None), P(Y))
    out_specs = (P(ROW_COL), P(ROW_COL, None), P(COL_ROW, None))
    return jax.shard_map(
        on_device, mesh=torus, in_specs=in_specs, out_specs=out_specs, check_vma=False
    )
```
